32 devices in a mesh: heads: 2 (over x), ctx: 16 (over z, y, core).
Axes of the slice: x: 2, y: 2, z: 4, core: 2. Of those that a mesh axis runs over, the one named last changes fastest.
Arguments:
- queries: bfloat16 [4096, 4096], P('ctx', 'heads'), may hold values from -80 to 80
- keys: bfloat16 [4096, 1024], P('ctx', 'heads'), may hold values from -4.5 to 4.5
- values: bfloat16 [4096, 1024], P('ctx', 'heads'), may hold values from -6 to 6
- doc_ids: int32 [4096], P('ctx'), may hold values from 0 to 3, never falling along the last dimension, each value on 1 to 2048 neighbouring positions
- out_weight: bfloat16 [4096, 4096], P('heads', 'ctx'), may hold values from -0.09375 to 0.09375
Outputs:
- mixed: bfloat16 [4096, 4096], P('ctx', 'heads')
The draws below stay inside these ranges and needn't reach their ends.
Inputs may be any that keep to these rules, and one draw needn't show every extreme that they name: `doc_ids`: document ids never fall along the tokens; each document has at most 2048 tokens.
All inputs are finite; a program needn't handle non-finite values.
Results may differ from the reference program's by a relative error of at most 0.015.
Values may be sent and summed in bfloat16 or wider, within the bound.
A program may use at most 64 MiB of HBM per device.

```python
import math
import jax
import jax.numpy as jnp
import numpy as np
from jax import lax

D = 4096
QH = 32
KEY_VALUE_HEADS = 8
HEAD_SIZE = 128
LOOKBACK_WINDOW = 4096
TOK_DEV = 256
QPG = 4
SEQUENCE_TOKENS = 4096
MOST_DOC = 2048


def shared_pair(key):
    key_k = jax.random.fold_in(key, 17)
    key_q = jax.random.fold_in(key, 29)
    kbase = jnp.clip(jax.random.normal(key_k, (SEQUENCE_TOKENS, KEY_VALUE_HEADS, HEAD_SIZE), jnp.float32), -4.0, 4.0)
    qbase = jnp.clip(jax.random.normal(key_q, (SEQUENCE_TOKENS, KEY_VALUE_HEADS, QH // KEY_VALUE_HEADS, HEAD_SIZE), jnp.float32), -4.0, 4.0)
    return (qbase, kbase)


def draw_queries(key, part):
    qbase, kbase = shared_pair(key)
    return qbase.reshape(SEQUENCE_TOKENS, QH * HEAD_SIZE).astype(jnp.bfloat16)


def draw_keys(key, part):
    qbase, kbase = shared_pair(key)
    return kbase.reshape(SEQUENCE_TOKENS, KEY_VALUE_HEADS * HEAD_SIZE).astype(jnp.bfloat16)


def block_scale(rng, extent, shards, least, high):
    def one(position, parts):
        draws = jax.random.uniform(jax.random.fold_in(jax.random.fold_in(rng, 6), position), (parts,), jnp.float32, least / len(shards), high / len(shards))
        return jnp.repeat(jnp.exp(draws), extent[position] // parts).reshape((-1,) + (1,) * (len(extent) - position - 1))

    factor_of = one(*shards[0])
    for cut in shards[1:]:
        factor_of = factor_of * one(*cut)
    return factor_of


def split_up(count, total, reach, lean):
    loads = [(1 << 20) // math.isqrt(standing ** lean) + 1 for standing in range(2, count + 1)]
    spare, given = total - reach - (count - 1), [1] * (count - 1)
    while spare > 0:
        movable = [i for i in range(count - 1) if given[i] < reach]
        mass, left = sum([loads[i] for i in movable]), spare
        for i in movable:
            extra = min(reach - given[i], max(1, left * loads[i] // mass), spare)
            given[i] = given[i] + extra
            spare = spare - extra
    return np.array([reach] + given)


def ragged(rng, amount, total, most, lean):
    if amount == 2:
        one = jax.random.randint(rng, (), max(1, total - most), min(most, total - 1) + 1)
        return jnp.stack([one, total - one])
    tallies = jnp.asarray(split_up(amount, total, most, lean), jnp.int32)
    pairs = (amount - 1) // 2
    source_of, receiver = tallies[1:1 + 2 * pairs:2], tallies[2:2 + 2 * pairs:2]
    room = jnp.minimum(source_of - 1, most - receiver)
    passed = jax.random.randint(jax.random.fold_in(rng, 1), (pairs,), 0, 1 << 20) % (room + 1)
    tallies = tallies.at[1:1 + 2 * pairs:2].set(source_of - passed).at[2:2 + 2 * pairs:2].set(receiver + passed)
    return tallies[jax.random.permutation(jax.random.fold_in(rng, 2), amount)]


def bell_draw(rng, extent, spread, bound, cuts=(), kind=jnp.bfloat16):
    entries = jax.random.normal(rng, extent, jnp.float32) * spread
    if len(cuts) > 0:
        entries = block_scale(rng, extent, cuts, -0.22, 0.18) * entries
    return jnp.clip(entries, min=-bound, max=bound).astype(kind)


def setup_inputs(seed: int = 0) -> dict:
    key_list = jax.random.split(jax.random.key(seed), 6)
    queries = draw_queries(jax.random.fold_in(key_list[5], 71), 0)
    keys = draw_keys(jax.random.fold_in(key_list[5], 71), 0)
    values = bell_draw(key_list[2], (SEQUENCE_TOKENS, KEY_VALUE_HEADS * HEAD_SIZE), 1.0, 6.0, ((0, 16), (1, 2)))
    doc_ids = jnp.searchsorted(jnp.cumsum(ragged(key_list[3], SEQUENCE_TOKENS // (4 * TOK_DEV), SEQUENCE_TOKENS, MOST_DOC, 2)), jnp.arange(SEQUENCE_TOKENS), side="right").astype(jnp.int32)
    out_weight = bell_draw(key_list[4], (QH * HEAD_SIZE, D), (QH * HEAD_SIZE) ** -0.5, 0.09375, ((0, 2), (1, 16)))
    return {"queries": queries, "keys": keys, "values": values, "doc_ids": doc_ids, "out_weight": out_weight}


def reference(queries, keys, values, doc_ids, out_weight):
    scale = HEAD_SIZE ** -0.5
    q = queries.reshape(SEQUENCE_TOKENS, KEY_VALUE_HEADS, QPG, HEAD_SIZE)
    kpad = jnp.concatenate([jnp.zeros((LOOKBACK_WINDOW, KEY_VALUE_HEADS * HEAD_SIZE), keys.dtype), keys], axis=0).reshape(SEQUENCE_TOKENS + LOOKBACK_WINDOW, KEY_VALUE_HEADS, HEAD_SIZE)
    value_padded = jnp.concatenate([jnp.zeros((LOOKBACK_WINDOW, KEY_VALUE_HEADS * HEAD_SIZE), values.dtype), values], axis=0).reshape(SEQUENCE_TOKENS + LOOKBACK_WINDOW, KEY_VALUE_HEADS, HEAD_SIZE)
    dpad = jnp.concatenate([jnp.full((LOOKBACK_WINDOW,), -1, jnp.int32), doc_ids.astype(jnp.int32)], axis=0)
    block = TOK_DEV
    window_extent = LOOKBACK_WINDOW + block

    def one(index):
        begin_offset = (index * block).astype(jnp.int32)
        qb = lax.dynamic_slice_in_dim(q, begin_offset, block, 0).astype(jnp.float32)
        kb = lax.dynamic_slice_in_dim(kpad, begin_offset, window_extent, 0).astype(jnp.float32)
        value_block = lax.dynamic_slice_in_dim(value_padded, begin_offset, window_extent, 0).astype(jnp.float32)
        dq = lax.dynamic_slice_in_dim(doc_ids.astype(jnp.int32), begin_offset, block, 0)
        dk = lax.dynamic_slice_in_dim(dpad, begin_offset, window_extent, 0)
        scores = jnp.einsum('tgnh,sgh->tgns', qb, kb) * scale
        qpos = begin_offset + jnp.arange(block, dtype=jnp.int32)
        kpos = begin_offset - LOOKBACK_WINDOW + jnp.arange(window_extent, dtype=jnp.int32)
        vis = (kpos[None, :] <= qpos[:, None]) & (qpos[:, None] - kpos[None, :] < LOOKBACK_WINDOW) & (kpos[None, :] >= 0) & (dq[:, None] == dk[None, :])
        vis = vis[:, None, None, :]
        scores = jnp.where(vis, scores, jnp.float32(-1e30))
        rowmax = jnp.max(scores, axis=-1, keepdims=True)
        weights = jnp.where(vis, jnp.exp(scores - rowmax), jnp.float32(0.0))
        total = jnp.sum(weights, axis=-1)
        rounded = weights.astype(jnp.bfloat16)
        out = jnp.einsum('tgns,sgh->tgnh', rounded.astype(jnp.float32), value_block) / total[..., None]
        return out.astype(jnp.bfloat16).reshape(block, KEY_VALUE_HEADS * QPG * HEAD_SIZE)

    attn = lax.map(one, jnp.arange(SEQUENCE_TOKENS // block, dtype=jnp.int32)).reshape(SEQUENCE_TOKENS, QH * HEAD_SIZE)
    return jnp.dot(attn, out_weight, preferred_element_type=jnp.float32).astype(jnp.bfloat16)
```

```python
import functools
import math

import jax
import jax.numpy as jnp
from jax import lax
from jax.experimental import pallas as pl
from jax.experimental.pallas import tpu as pltpu
from jax.sharding import PartitionSpec as P

HEAD_SIZE = 128
LOOKBACK_WINDOW = 4096
QPG = 4


PLANE = 4
DOC_ROWS = 16
MESH = pl.DeviceIdType.MESH


MASKED = 131072.0


def fused_kernel(
    planes, n_heads, groups, tok, wcols,
    q_ref, docs_ref, k_hbm, v_hbm, w_hbm, out_ref,
    kvbuf, feat, qfeat, wbuf, abuf, acc, rowmax, xsend, xrecv, keep, rsend, obuf,
    local_sem, kv_recv, kvz_send, kvp_send, kvf_send,
    w_recv, w_right, w_left, a_recv, a_send, a_fwd,
    x_send, x_recv, o_send, o_recv,
):
    h = lax.axis_index("heads")
    c = lax.axis_index("ctx")
    z = c // PLANE
    p = c % PLANE
    core = p % 2
    row = p // 2
    mate = p + 1 - 2 * core
    across = (p + 2) % PLANE
    diag = (mate + 2) % PLANE
    last = planes - 1
    per_half = planes // n_heads
    half = wcols // 2
    pair = groups // 2
    part_heads = QPG * pair
    kcols = pair * HEAD_SIZE
    acols = part_heads * HEAD_SIZE
    bf, f32 = jnp.bfloat16, jnp.float32

    def in_plane(other):
        return (h, z * PLANE + other)

    up = (h, c + PLANE)
    down = (h, c - PLANE)

    def copy(src, dst, send, recv, dev):
        return pltpu.make_async_remote_copy(
            src_ref=src, dst_ref=dst, send_sem=send, recv_sem=recv,
            device_id=dev, device_id_type=MESH,
        )

    def kv_up(d, s):
        return copy(
            kvbuf.at[d, p, s], kvbuf.at[d + 1, p, s], kvz_send.at[d, s],
            kv_recv.at[d + 1, p, s], up,
        )

    def kv_side(d, which, s):
        dev = in_plane(mate if which == 0 else across)
        ref = kvbuf.at[d, p, s]
        return copy(ref, ref, kvp_send.at[d, which, s], kv_recv.at[d, p, s], dev)

    def kv_forward(d, s):
        ref = kvbuf.at[d, across, s]
        return copy(ref, ref, kvf_send.at[d, s], kv_recv.at[d, across, s], in_plane(mate))

    def kv_wait(d, who, s):
        ref = kvbuf.at[d, who, s]
        copy(ref, ref, kvf_send.at[d, s], kv_recv.at[d, who, s], in_plane(mate)).wait_recv()

    def w_up(j, s):
        ref = wbuf.at[j, s]
        return copy(ref, ref, w_right.at[j, s], w_recv.at[j, s], up)

    def w_down(j, s):
        ref = wbuf.at[j, s]
        return copy(ref, ref, w_left.at[j, s], w_recv.at[j, s], down)

    def arrive(j, s):
        ref = wbuf.at[j, s]
        copy(ref, ref, w_left.at[j, s], w_recv.at[j, s], in_plane(mate)).wait_recv()

        @pl.when((j > z) & (z > 0))
        def _():
            w_down(j, s).start()

        @pl.when((j < z) & (z < last))
        def _():
            w_up(j, s).start()

    def target(k):
        return jnp.where(k == 0, across, jnp.where(k == 1, diag, jnp.where(k == 2, mate, p)))

    def a_part(who, s):
        return abuf.at[who, s]

    def a_side(which, s):
        dev = in_plane(mate if which == 0 else across)
        return copy(a_part(p, s), a_part(p, s), a_send.at[which, s], a_recv.at[p, s], dev)

    def a_forward(s):
        return copy(
            a_part(across, s), a_part(across, s), a_fwd.at[s], a_recv.at[across, s], in_plane(mate)
        )

    def a_wait(who, s):
        copy(
            a_part(who, s), a_part(who, s), a_fwd.at[s], a_recv.at[who, s], in_plane(mate)
        ).wait_recv()

    def x_copy(u, pp):
        return copy(
            xsend.at[u, pp], xrecv.at[u, pp], x_send.at[u, pp], x_recv.at[u, pp], (1 - h, c)
        )

    def o_copy(u, pp):
        return copy(
            rsend.at[u, pp], obuf.at[u, p], o_send.at[u, pp], o_recv.at[u, p], in_plane(pp)
        )

    kv_in = []
    for s in range(2):
        cols = slice(s * kcols, (s + 1) * kcols)
        mine = kvbuf.at[0, p, s]
        kv_in.append([
            pltpu.make_async_copy(
                k_hbm.at[:, cols], mine.at[0:tok, 0:kcols], local_sem.at[3 * s]
            ),
            pltpu.make_async_copy(
                v_hbm.at[:, cols], mine.at[0:tok, kcols : 2 * kcols], local_sem.at[3 * s + 1]
            ),
            pltpu.make_async_copy(
                docs_ref, mine.at[tok : tok + DOC_ROWS, :], local_sem.at[3 * s + 2]
            ),
        ])
    w_in = [
        pltpu.make_async_copy(
            w_hbm.at[:, s * half : (s + 1) * half], wbuf.at[z, s], local_sem.at[6 + s]
        )
        for s in range(2)
    ]
    for s in range(2):
        for one in kv_in[s]:
            one.start()
    w_in[0].start()
    w_in[1].start()

    barrier = pltpu.get_barrier_semaphore()
    for dev in (in_plane(mate), in_plane(across), in_plane(diag), (1 - h, c)):
        pl.semaphore_signal(barrier, inc=1, device_id=dev, device_id_type=MESH)

    @pl.when(z < last)
    def _():
        pl.semaphore_signal(barrier, inc=1, device_id=up, device_id_type=MESH)

    @pl.when(z > 0)
    def _():
        pl.semaphore_signal(barrier, inc=1, device_id=down, device_id_type=MESH)

    pl.semaphore_wait(barrier, 4 + jnp.minimum(z, 1) + jnp.minimum(last - z, 1))

    for s in range(2):
        for one in kv_in[s]:
            one.wait()

        @pl.when(z < last)
        def _():
            kv_up(0, s).start()

        @pl.when(row == 0)
        def _():
            kv_side(0, 1, s).start()

        @pl.when(core == 0)
        def _():
            kv_side(0, 0, s).start()

    for s in range(2):
        w_in[s].wait()

        @pl.when(z > 0)
        def _():
            w_down(z, s).start()

        @pl.when(z == 0)
        def _():
            w_up(z, s).start()

    factor = HEAD_SIZE ** (-0.5) * math.log2(math.e)

    def same_lane(d, who):
        docs = kvbuf[d, who, 0, tok : tok + DOC_ROWS, 0:tok].astype(f32)[0:1, :]
        column = jnp.broadcast_to(docs, (HEAD_SIZE, tok)).T
        return column == lax.broadcasted_iota(jnp.int32, (tok, HEAD_SIZE), 1).astype(f32)

    def mark(d, lo, count):
        def one(k, carry):
            hit = same_lane(d, lo + k)
            feat[d, lo + k] = jnp.where(hit, jnp.float32(1.0), jnp.float32(0.0)).astype(bf)
            return carry

        lax.fori_loop(0, count, one, 0)

    def attend(d, lo, blocks, s, first):
        ones = jnp.ones((tok, HEAD_SIZE), bf)
        lanes = 2 * HEAD_SIZE
        heads, keys, vals = [], [], []
        for u in range(pair):
            kc = slice(u * HEAD_SIZE, (u + 1) * HEAD_SIZE)
            vc = slice(kcols + u * HEAD_SIZE, kcols + (u + 1) * HEAD_SIZE)
            kb = [
                jnp.concatenate([kvbuf[d, lo + b, s, 0:tok, kc], feat[d, lo + b]], axis=1)
                for b in range(blocks)
            ]
            vb = [
                jnp.concatenate([kvbuf[d, lo + b, s, 0:tok, vc], ones], axis=1)
                for b in range(blocks)
            ]
            for n in range(QPG):
                heads.append(s * part_heads + u * QPG + n)
                keys.append(kb)
                vals.append(vb)
        keys = [jnp.concatenate(kb, axis=0) if blocks > 1 else kb[0] for kb in keys]
        vals = [jnp.concatenate(vb, axis=0) if blocks > 1 else vb[0] for vb in vals]
        if not first:
            olds = [rowmax[head] for head in heads]
            accs = [acc[head] for head in heads]
        done = []
        for n, head in enumerate(heads):
            cols = pl.ds(pl.multiple_of(head * HEAD_SIZE, HEAD_SIZE), HEAD_SIZE)
            qs = jnp.concatenate([q_ref[:, cols], qfeat[...]], axis=1)
            scores = lax.dot_general(
                qs, keys[n], (((1,), (1,)), ((), ())), preferred_element_type=f32
            )
            if first:
                qpos = lax.broadcasted_iota(jnp.int32, (tok, tok), 0)
                kpos = lax.broadcasted_iota(jnp.int32, (tok, tok), 1)
                scores = jnp.where(kpos <= qpos, scores, jnp.float32(-1e30))
            top = functools.reduce(
                jnp.maximum,
                [scores[:, i : i + HEAD_SIZE] for i in range(0, blocks * tok, HEAD_SIZE)],
            )
            top = jnp.max(top, axis=1, keepdims=True)
            if not first:
                top = jnp.maximum(top, olds[n][:, 0:1])
            weights = jnp.exp2((scores - top) * factor).astype(bf)
            both = jnp.dot(weights, vals[n], preferred_element_type=f32)
            if not first:
                shrink = jnp.exp2((olds[n] - top) * factor)
                both = accs[n] * jnp.concatenate([shrink, shrink], axis=1) + both
            done.append((jnp.broadcast_to(top, (tok, HEAD_SIZE)), both))
        for head, (top, both) in zip(heads, done):
            rowmax[head] = top
            acc[head] = both

    def attend_some(d, lo, count, s, most):
        for blocks in range(1, most + 1):

            @pl.when(count == blocks)
            def _():
                attend(d, lo, blocks, s, False)

    qfeat[...] = jnp.where(same_lane(0, p), jnp.float32(0.0), jnp.float32(-MASKED)).astype(bf)
    mark(0, p, 1)

    def own_half(s, carry):
        attend(0, p, 1, s, True)
        return carry

    lax.fori_loop(0, 2, own_half, 0)

    @pl.when(z > 0)
    def _():
        for s in range(2):
            kv_wait(1, p, s)

            @pl.when(z < last)
            def _():
                kv_up(1, s).start()

            kv_side(1, 1, s).start()
            kv_side(1, 0, s).start()

        @pl.when(z < last)
        def _():
            w_up(z, 0).start()
            w_up(z, 1).start()

    def first_plane(s, carry):
        @pl.when(row == 1)
        def _():
            kv_wait(0, across, s)
            kv_forward(0, s).start()

        @pl.when(core == 1)
        def _():
            kv_wait(0, mate, s)

        @pl.when(row == 1)
        def _():
            kv_wait(0, diag, s)

        @pl.when(s == 0)
        def _():
            mark(0, 0, p)

        attend_some(0, 0, p, s, PLANE - 1)
        return carry

    lax.fori_loop(0, 2, first_plane, 0)

    def second_plane(s, carry):
        @pl.when(z < last)
        def _():
            arrive(z + 1, s)

        @pl.when(z > 1)
        def _():
            kv_wait(2, p, s)

            @pl.when(row == 1)
            def _():
                kv_side(2, 1, s).start()

            @pl.when(core == 1)
            def _():
                kv_side(2, 0, s).start()

        @pl.when(z > 0)
        def _():
            kv_wait(1, across, s)
            kv_forward(1, s).start()
            kv_wait(1, mate, s)
            kv_wait(1, diag, s)

            @pl.when(s == 0)
            def _():
                mark(1, 0, PLANE)

            attend(1, 0, PLANE, s, False)

        return carry

    lax.fori_loop(0, 2, second_plane, 0)

    def third_plane(s, carry):
        @pl.when(z > 1)
        def _():
            @pl.when(row == 0)
            def _():
                kv_wait(2, across, s)
                kv_forward(2, s).start()

            @pl.when(core == 0)
            def _():
                kv_wait(2, mate, s)

            @pl.when(row == 0)
            def _():
                kv_wait(2, diag, s)

            @pl.when(s == 0)
            def _():
                mark(2, p, PLANE - p)

            attend_some(2, p, PLANE - p, s, PLANE)

        for n in range(part_heads):
            both = acc[s * part_heads + n]
            attn = both[:, 0:HEAD_SIZE] / both[:, HEAD_SIZE : 2 * HEAD_SIZE]
            abuf[p, s, :, n * HEAD_SIZE : (n + 1) * HEAD_SIZE] = attn.astype(bf)
        a_side(1, s).start()
        a_side(0, s).start()
        return carry

    lax.fori_loop(0, 2, third_plane, 0)

    def order(i):
        if i == 0:
            return z
        if i == 1:
            return jnp.where(z < last, z + 1, z - 1)
        if i == 2:
            return jnp.where(z == 0, 2, jnp.where(z == last, last - 2, z - 1))
        return jnp.where(z < 2, last, 0)

    def place(u, pp, part):
        mine = ((u // 2) // per_half) == h
        uu = u % (2 * per_half)

        @pl.when(mine)
        def _():
            keep[uu, pp] = part

        @pl.when(jnp.logical_not(mine))
        def _():
            xsend[uu, pp] = part.astype(bf)
            x_copy(uu, pp).start()

    def attn_of(pp):
        return jnp.concatenate([abuf[pp, 0], abuf[pp, 1]], axis=1)

    def project(j, lo, hi):
        def rows(k, carry):
            pp = target(k)
            both = jnp.concatenate([wbuf[j, 0], wbuf[j, 1]], axis=1)
            part = jnp.dot(attn_of(pp), both, preferred_element_type=f32)
            place(2 * j, pp, part[:, :half])
            place(2 * j + 1, pp, part[:, half:])
            return carry

        lax.fori_loop(lo, hi, rows, 0)

    def project_half(j, s):
        def rows(k, carry):
            pp = target(k)
            part = jnp.dot(attn_of(pp), wbuf[j, s], preferred_element_type=f32)
            place(2 * j + s, pp, part)
            return carry

        lax.fori_loop(0, PLANE, rows, 0)

    def column(u, src):
        return pl.ds(pl.multiple_of(((u // 2) * PLANE + src) * wcols + (u % 2) * half, half), half)

    def finish(j, s):
        @pl.when((j // per_half) == h)
        def _():
            u = (2 * j + s) % (2 * per_half)

            def rows(k, carry):
                pp = target(k)
                x_copy(u, pp).wait_recv()
                done = (keep[u, pp] + xrecv[u, pp].astype(f32)).astype(bf)

                @pl.when(pp == p)
                def _():
                    out_ref[:, column(u, p)] = done

                @pl.when(pp != p)
                def _():
                    rsend[u, pp] = done
                    o_copy(u, pp).start()

                return carry

            lax.fori_loop(0, PLANE, rows, 0)

    def finish_all(j):
        def one(s, carry):
            finish(j, s)
            return carry

        lax.fori_loop(0, 2, one, 0)

    a_wait(mate, 0)
    a_wait(mate, 1)
    project(order(0), 2, PLANE)

    @pl.when(z == last)
    def _():
        arrive(order(1), 0)
        arrive(order(1), 1)

    project(order(1), 2, PLANE)

    @pl.when(z < last)
    def _():
        arrive(order(2), 0)
        arrive(order(2), 1)
        project(order(2), 2, PLANE)

    @pl.when((z > 0) & (z < last))
    def _():
        arrive(order(3), 0)

    @pl.when(z == 1)
    def _():
        arrive(order(3), 1)

    for s in range(2):
        a_wait(across, s)
        a_forward(s).start()
    for s in range(2):
        a_wait(diag, s)
    project(order(0), 0, 2)
    project(order(1), 0, 2)

    @pl.when(z < last)
    def _():
        project(order(2), 0, 2)

        @pl.when(z == 0)
        def _():
            arrive(order(3), 0)

        @pl.when(z != 1)
        def _():
            arrive(order(3), 1)

        project(order(3), 0, PLANE)
        for i in range(PLANE):
            finish_all(order(i))

    @pl.when(z == last)
    def _():
        arrive(order(2), 0)
        arrive(order(2), 1)
        project(order(2), 0, PLANE)
        finish_all(order(0))
        finish_all(order(1))
        arrive(order(3), 0)
        project_half(order(3), 0)
        finish_all(order(2))
        arrive(order(3), 1)
        project_half(order(3), 1)
        finish_all(order(3))

    def collect(k, carry):
        u = k // PLANE
        src = k % PLANE

        @pl.when(src != p)
        def _():
            copy(
                obuf.at[u, src], obuf.at[u, src], o_send.at[u, src], o_recv.at[u, src],
                in_plane(mate),
            ).wait_recv()
            out_ref[:, column(u, src)] = obuf[u, src]
            o_copy(u, src).wait_send()

        x_copy(u, src).wait_send()
        return carry

    lax.fori_loop(0, 2 * per_half * PLANE, collect, 0)

    for s in range(2):
        a_side(0, s).wait_send()
        a_side(1, s).wait_send()
        a_forward(s).wait_send()

    def w_drain(j, carry):
        @pl.when((j <= z) & (z < last))
        def _():
            w_up(j, 0).wait_send()
            w_up(j, 1).wait_send()

        @pl.when((j >= z) & (z > 0))
        def _():
            w_down(j, 0).wait_send()
            w_down(j, 1).wait_send()

        return carry

    lax.fori_loop(0, planes, w_drain, 0)

    for s in range(2):
        @pl.when(z < last)
        def _():
            kv_up(0, s).wait_send()

            @pl.when(z > 0)
            def _():
                kv_up(1, s).wait_send()

        @pl.when(row == 0)
        def _():
            kv_side(0, 1, s).wait_send()

        @pl.when(core == 0)
        def _():
            kv_side(0, 0, s).wait_send()

        @pl.when(row == 1)
        def _():
            kv_forward(0, s).wait_send()

        @pl.when(z > 0)
        def _():
            kv_side(1, 0, s).wait_send()
            kv_side(1, 1, s).wait_send()
            kv_forward(1, s).wait_send()

        @pl.when(z > 1)
        def _():
            @pl.when(row == 1)
            def _():
                kv_side(2, 1, s).wait_send()

            @pl.when(core == 1)
            def _():
                kv_side(2, 0, s).wait_send()

            @pl.when(row == 0)
            def _():
                kv_forward(2, s).wait_send()


def fused_body(n_ctx, n_heads, queries, keys, values, doc_ids, out_weight):
    tok, qcols = queries.shape
    kdim = keys.shape[1]
    groups = kdim // HEAD_SIZE
    krows, wcols = out_weight.shape
    planes = n_ctx // PLANE
    span = QPG * groups
    per_half = planes // n_heads
    docs = jnp.broadcast_to(
        jnp.pad(doc_ids.astype(jnp.bfloat16), (0, kdim - tok))[None, :], (DOC_ROWS, kdim)
    )
    bf, f32 = jnp.bfloat16, jnp.float32
    dma = pltpu.SemaphoreType.DMA
    anywhere = pl.BlockSpec(memory_space=pl.ANY)
    return pl.pallas_call(
        functools.partial(fused_kernel, planes, n_heads, groups, tok, wcols),
        out_shape=jax.ShapeDtypeStruct((tok, per_half * PLANE * wcols), bf),
        in_specs=[pl.BlockSpec(memory_space=pltpu.VMEM), anywhere, anywhere, anywhere, anywhere],
        out_specs=pl.BlockSpec(memory_space=pltpu.VMEM),
        scratch_shapes=[
            pltpu.VMEM((3, PLANE, 2, tok + DOC_ROWS, kdim), bf),
            pltpu.VMEM((3, PLANE, tok, HEAD_SIZE), bf),
            pltpu.VMEM((tok, HEAD_SIZE), bf),
            pltpu.VMEM((planes, 2, krows, wcols // 2), bf),
            pltpu.VMEM((PLANE, 2, tok, krows // 2), bf),
            pltpu.VMEM((span, tok, 2 * HEAD_SIZE), f32),
            pltpu.VMEM((span, tok, HEAD_SIZE), f32),
            pltpu.VMEM((2 * per_half, PLANE, tok, wcols // 2), bf),
            pltpu.VMEM((2 * per_half, PLANE, tok, wcols // 2), bf),
            pltpu.VMEM((2 * per_half, PLANE, tok, wcols // 2), f32),
            pltpu.VMEM((2 * per_half, PLANE, tok, wcols // 2), bf),
            pltpu.VMEM((2 * per_half, PLANE, tok, wcols // 2), bf),
            dma((8,)),
            dma((3, PLANE, 2)),
            dma((2, 2)),
            dma((3, 2, 2)),
            dma((3, 2)),
            dma((planes, 2)),
            dma((planes, 2)),
            dma((planes, 2)),
            dma((PLANE, 2)),
            dma((2, 2)),
            dma((2,)),
            dma((2 * per_half, PLANE)),
            dma((2 * per_half, PLANE)),
            dma((2 * per_half, PLANE)),
            dma((2 * per_half, PLANE)),
        ],
        compiler_params=pltpu.CompilerParams(
            collective_id=0, has_side_effects=True, vmem_limit_bytes=56 * 1024 * 1024
        ),
    )(queries, docs, keys, values, out_weight)


def fits_fused(n_ctx, n_heads, queries, keys, out_weight):
    tokens = queries.shape[0]
    tok = tokens // n_ctx
    reach = min(LOOKBACK_WINDOW, tokens // 2)
    return (
        n_heads == 2
        and n_ctx % PLANE == 0
        and n_ctx // PLANE == 4
        and tok == 2 * HEAD_SIZE
        and reach == 2 * PLANE * tok
        and reach < LOOKBACK_WINDOW
        and keys.shape[1] // n_heads >= tok
        and (out_weight.shape[1] // n_ctx) % 256 == 0
        and keys.shape[1] // n_heads % (2 * HEAD_SIZE) == 0
    )


def passed_along(block, axis, distance):
    devices = range(lax.axis_size(axis))
    route = [(i - distance, i) for i in devices if i - distance in devices]
    return lax.ppermute(block, axis, route)


def body(queries, keys, values, doc_ids, out_weight):
    tok_rows = queries.shape[0]
    groups = keys.shape[1] // HEAD_SIZE
    scale = HEAD_SIZE ** (-0.5)
    q_local = queries.reshape(tok_rows, groups, QPG, HEAD_SIZE)
    here = lax.axis_index("ctx")
    qpos = here * tok_rows + jnp.arange(tok_rows, dtype=jnp.int32)
    reach = LOOKBACK_WINDOW // tok_rows

    def work(state, kblk, vblk, sblk, kstart):
        rowmax, total, accum = state
        scores = (
            jnp.einsum(
                "tgnh,sgh->tgns",
                q_local,
                kblk.reshape(tok_rows, groups, HEAD_SIZE),
                preferred_element_type=jnp.float32,
            )
            * scale
        )
        kpos = kstart + jnp.arange(tok_rows, dtype=jnp.int32)
        vis = (
            (kpos[None, :] <= qpos[:, None])
            & (qpos[:, None] - kpos[None, :] < LOOKBACK_WINDOW)
            & (kpos[None, :] >= 0)
            & (doc_ids[:, None] == sblk[None, :])
        )
        vis = vis[:, None, None, :]
        scores = jnp.where(vis, scores, jnp.float32(-1e30))
        newmax = jnp.maximum(rowmax, jnp.max(scores, axis=-1))
        weights = jnp.where(vis, jnp.exp(scores - newmax[..., None]), jnp.float32(0.0))
        factor = jnp.exp(rowmax - newmax)
        total = total * factor + jnp.sum(weights, axis=-1)
        rounded = weights.astype(jnp.bfloat16)
        contrib = jnp.einsum(
            "tgns,sgh->tgnh",
            rounded,
            vblk.reshape(tok_rows, groups, HEAD_SIZE),
            preferred_element_type=jnp.float32,
        )
        accum = accum * factor[..., None] + contrib
        return (newmax, total, accum)

    def attend(state, kblk, vblk, sblk, kstart):
        return work(state, kblk, vblk, sblk, kstart)

    state = (
        jnp.full((tok_rows, groups, QPG), -1e30, jnp.float32),
        jnp.zeros((tok_rows, groups, QPG), jnp.float32),
        jnp.zeros((tok_rows, groups, QPG, HEAD_SIZE), jnp.float32),
    )
    state = attend(state, keys, values, doc_ids, here * tok_rows)

    def chain_step(depth, carry):
        st, kblk, vblk, sblk = carry
        kblk, vblk, sblk = passed_along((kblk, vblk, sblk), "ctx", 1)
        st = attend(st, kblk, vblk, sblk, (here - depth) * tok_rows)
        return (st, kblk, vblk, sblk)

    state = lax.fori_loop(1, reach + 1, chain_step, (state, keys, values, doc_ids))[0]
    rowmax, total, accum = state
    attn = (
        (accum / total[..., None]).astype(jnp.bfloat16).reshape(tok_rows, groups * QPG * HEAD_SIZE)
    )
    partial_sums = jnp.dot(
        attn,
        lax.all_gather(out_weight, "ctx", axis=1, tiled=True),
        preferred_element_type=jnp.float32,
    )
    return lax.psum_scatter(
        partial_sums.astype(jnp.bfloat16), "heads", scatter_dimension=1, tiled=True
    )


def solution(mesh):
    in_specs = (
        P("ctx", "heads"),
        P("ctx", "heads"),
        P("ctx", "heads"),
        P("ctx"),
        P("heads", "ctx"),
    )
    out_specs = P("ctx", "heads")

    def run(queries, keys, values, doc_ids, out_weight):
        n_ctx, n_heads = mesh.shape["ctx"], mesh.shape["heads"]
        local = body
        if fits_fused(n_ctx, n_heads, queries, keys, out_weight):
            local = functools.partial(fused_body, n_ctx, n_heads)
        return jax.shard_map(
            local, mesh=mesh, in_specs=in_specs, out_specs=out_specs, check_vma=False
        )(queries, keys, values, doc_ids, out_weight)

    return run
```

```python
import functools
import math

import jax
import jax.numpy as jnp
from jax import lax
from jax.experimental import pallas as pl
from jax.experimental.pallas import tpu as pltpu
from jax.sharding import PartitionSpec as P

HEAD_SIZE = 128
LOOKBACK_WINDOW = 4096
QPG = 4


PLANE = 4
DOC_ROWS = 16
MESH = pl.DeviceIdType.MESH


MASKED = 131072.0


def fused_kernel(
    planes, n_heads, groups, tok, wcols,
    q_ref, docs_ref, k_hbm, v_hbm, w_hbm, out_ref,
    kvbuf, feat, qfeat, wbuf, abuf, lent, acc, rowmax, xsend, xrecv, keep, rsend, obuf,
    psend, precv,
    local_sem, kv_recv, kvz_send, kvp_send, kvf_send,
    w_recv, w_right, w_left, a_recv, a_send, a_fwd,
    x_send, x_recv, o_send, o_recv,
    l_recv, l_down, l_mate, l_across, p_send, p_recv,
):
    h = lax.axis_index("heads")
    c = lax.axis_index("ctx")
    z = c // PLANE
    p = c % PLANE
    core = p % 2
    row = p // 2
    mate = p + 1 - 2 * core
    across = (p + 2) % PLANE
    diag = (mate + 2) % PLANE
    last = planes - 1
    helper = last - 1
    per_half = planes // n_heads
    half = wcols // 2
    pair = groups // 2
    part_heads = QPG * pair
    kcols = pair * HEAD_SIZE
    acols = part_heads * HEAD_SIZE
    bf, f32 = jnp.bfloat16, jnp.float32

    def in_plane(other):
        return (h, z * PLANE + other)

    up = (h, c + PLANE)
    down = (h, c - PLANE)

    def copy(src, dst, send, recv, dev):
        return pltpu.make_async_remote_copy(
            src_ref=src, dst_ref=dst, send_sem=send, recv_sem=recv,
            device_id=dev, device_id_type=MESH,
        )

    def kv_up(d, s):
        return copy(
            kvbuf.at[d, p, s], kvbuf.at[d + 1, p, s], kvz_send.at[d, s],
            kv_recv.at[d + 1, p, s], up,
        )

    def kv_side(d, which, s):
        dev = in_plane(mate if which == 0 else across)
        ref = kvbuf.at[d, p, s]
        return copy(ref, ref, kvp_send.at[d, which, s], kv_recv.at[d, p, s], dev)

    def kv_forward(d, s):
        ref = kvbuf.at[d, across, s]
        return copy(ref, ref, kvf_send.at[d, s], kv_recv.at[d, across, s], in_plane(mate))

    def kv_wait(d, who, s):
        ref = kvbuf.at[d, who, s]
        copy(ref, ref, kvf_send.at[d, s], kv_recv.at[d, who, s], in_plane(mate)).wait_recv()

    def w_up(j, s):
        ref = wbuf.at[j, s]
        return copy(ref, ref, w_right.at[j, s], w_recv.at[j, s], up)

    def w_down(j, s):
        ref = wbuf.at[j, s]
        return copy(ref, ref, w_left.at[j, s], w_recv.at[j, s], down)

    def arrive(j, s):
        ref = wbuf.at[j, s]
        copy(ref, ref, w_left.at[j, s], w_recv.at[j, s], in_plane(mate)).wait_recv()

        @pl.when((j > z) & (z > 0))
        def _():
            w_down(j, s).start()

        @pl.when((j < z) & ((z < helper) | ((z == helper) & (j > 0))))
        def _():
            w_up(j, s).start()

    def target(k):
        return jnp.where(k == 0, across, jnp.where(k == 1, diag, jnp.where(k == 2, mate, p)))

    def a_part(who, s):
        return abuf.at[who, s]

    def a_side(which, s):
        dev = in_plane(mate if which == 0 else across)
        return copy(a_part(p, s), a_part(p, s), a_send.at[which, s], a_recv.at[p, s], dev)

    def a_forward(s):
        return copy(
            a_part(across, s), a_part(across, s), a_fwd.at[s], a_recv.at[across, s], in_plane(mate)
        )

    def a_wait(who, s):
        copy(
            a_part(who, s), a_part(who, s), a_fwd.at[s], a_recv.at[who, s], in_plane(mate)
        ).wait_recv()

    def lend_down(who, s, slot):
        return copy(a_part(who, s), lent.at[who, s], l_down.at[slot], l_recv.at[who, s], down)

    def lend_mate(who, s, slot):
        ref = lent.at[who, s]
        return copy(ref, ref, l_mate.at[slot], l_recv.at[who, s], in_plane(mate))

    def lend_across():
        ref = lent.at[p, 1]
        return copy(ref, ref, l_across, l_recv.at[p, 1], in_plane(across))

    def lend_wait(who, s):
        ref = lent.at[who, s]
        copy(ref, ref, l_mate.at[0], l_recv.at[who, s], in_plane(mate)).wait_recv()

    def give_back(pp):
        return copy(psend.at[pp], precv.at[pp], p_send.at[pp], p_recv.at[pp], up)

    def x_copy(u, pp):
        return copy(
            xsend.at[u, pp], xrecv.at[u, pp], x_send.at[u, pp], x_recv.at[u, pp], (1 - h, c)
        )

    def o_copy(u, pp):
        return copy(
            rsend.at[u, pp], obuf.at[u, p], o_send.at[u, pp], o_recv.at[u, p], in_plane(pp)
        )

    kv_in = []
    for s in range(2):
        cols = slice(s * kcols, (s + 1) * kcols)
        mine = kvbuf.at[0, p, s]
        kv_in.append([
            pltpu.make_async_copy(
                k_hbm.at[:, cols], mine.at[0:tok, 0:kcols], local_sem.at[3 * s]
            ),
            pltpu.make_async_copy(
                v_hbm.at[:, cols], mine.at[0:tok, kcols : 2 * kcols], local_sem.at[3 * s + 1]
            ),
            pltpu.make_async_copy(
                docs_ref, mine.at[tok : tok + DOC_ROWS, :], local_sem.at[3 * s + 2]
            ),
        ])
    w_in = [
        pltpu.make_async_copy(
            w_hbm.at[:, s * half : (s + 1) * half], wbuf.at[z, s], local_sem.at[6 + s]
        )
        for s in range(2)
    ]
    for s in range(2):
        for one in kv_in[s]:
            one.start()
    w_in[0].start()
    w_in[1].start()

    barrier = pltpu.get_barrier_semaphore()
    for dev in (in_plane(mate), in_plane(across), in_plane(diag), (1 - h, c)):
        pl.semaphore_signal(barrier, inc=1, device_id=dev, device_id_type=MESH)

    @pl.when(z < last)
    def _():
        pl.semaphore_signal(barrier, inc=1, device_id=up, device_id_type=MESH)

    @pl.when(z > 0)
    def _():
        pl.semaphore_signal(barrier, inc=1, device_id=down, device_id_type=MESH)

    pl.semaphore_wait(barrier, 4 + jnp.minimum(z, 1) + jnp.minimum(last - z, 1))

    for s in range(2):
        for one in kv_in[s]:
            one.wait()

        @pl.when(z < last)
        def _():
            kv_up(0, s).start()

        @pl.when(row == 0)
        def _():
            kv_side(0, 1, s).start()

        @pl.when(core == 0)
        def _():
            kv_side(0, 0, s).start()

    for s in range(2):
        w_in[s].wait()

        @pl.when(z > 0)
        def _():
            w_down(z, s).start()

        @pl.when(z == 0)
        def _():
            w_up(z, s).start()

    factor = HEAD_SIZE ** (-0.5) * math.log2(math.e)

    def same_lane(d, who):
        docs = kvbuf[d, who, 0, tok : tok + DOC_ROWS, 0:tok].astype(f32)[0:1, :]
        column = jnp.broadcast_to(docs, (HEAD_SIZE, tok)).T
        return column == lax.broadcasted_iota(jnp.int32, (tok, HEAD_SIZE), 1).astype(f32)

    def mark(d, lo, count):
        def one(k, carry):
            hit = same_lane(d, lo + k)
            feat[d, lo + k] = jnp.where(hit, jnp.float32(1.0), jnp.float32(0.0)).astype(bf)
            return carry

        lax.fori_loop(0, count, one, 0)

    def attend(d, lo, blocks, s, first):
        ones = jnp.ones((tok, HEAD_SIZE), bf)
        lanes = 2 * HEAD_SIZE
        heads, keys, vals = [], [], []
        for u in range(pair):
            kc = slice(u * HEAD_SIZE, (u + 1) * HEAD_SIZE)
            vc = slice(kcols + u * HEAD_SIZE, kcols + (u + 1) * HEAD_SIZE)
            kb = [
                jnp.concatenate([kvbuf[d, lo + b, s, 0:tok, kc], feat[d, lo + b]], axis=1)
                for b in range(blocks)
            ]
            vb = [
                jnp.concatenate([kvbuf[d, lo + b, s, 0:tok, vc], ones], axis=1)
                for b in range(blocks)
            ]
            for n in range(QPG):
                heads.append(s * part_heads + u * QPG + n)
                keys.append(kb)
                vals.append(vb)
        keys = [jnp.concatenate(kb, axis=0) if blocks > 1 else kb[0] for kb in keys]
        vals = [jnp.concatenate(vb, axis=0) if blocks > 1 else vb[0] for vb in vals]
        if not first:
            olds = [rowmax[head] for head in heads]
            accs = [acc[head] for head in heads]
        done = []
        for n, head in enumerate(heads):
            cols = pl.ds(pl.multiple_of(head * HEAD_SIZE, HEAD_SIZE), HEAD_SIZE)
            qs = jnp.concatenate([q_ref[:, cols], qfeat[...]], axis=1)
            scores = lax.dot_general(
                qs, keys[n], (((1,), (1,)), ((), ())), preferred_element_type=f32
            )
            if first:
                qpos = lax.broadcasted_iota(jnp.int32, (tok, tok), 0)
                kpos = lax.broadcasted_iota(jnp.int32, (tok, tok), 1)
                scores = jnp.where(kpos <= qpos, scores, jnp.float32(-1e30))
            top = functools.reduce(
                jnp.maximum,
                [scores[:, i : i + HEAD_SIZE] for i in range(0, blocks * tok, HEAD_SIZE)],
            )
            top = jnp.max(top, axis=1, keepdims=True)
            if not first:
                top = jnp.maximum(top, olds[n][:, 0:1])
            weights = jnp.exp2((scores - top) * factor).astype(bf)
            both = jnp.dot(weights, vals[n], preferred_element_type=f32)
            if not first:
                shrink = jnp.exp2((olds[n] - top) * factor)
                both = accs[n] * jnp.concatenate([shrink, shrink], axis=1) + both
            done.append((jnp.broadcast_to(top, (tok, HEAD_SIZE)), both))
        for head, (top, both) in zip(heads, done):
            rowmax[head] = top
            acc[head] = both

    def attend_some(d, lo, count, s, most):
        for blocks in range(1, most + 1):

            @pl.when(count == blocks)
            def _():
                attend(d, lo, blocks, s, False)

    qfeat[...] = jnp.where(same_lane(0, p), jnp.float32(0.0), jnp.float32(-MASKED)).astype(bf)
    mark(0, p, 1)

    def own_half(s, carry):
        attend(0, p, 1, s, True)
        return carry

    lax.fori_loop(0, 2, own_half, 0)

    @pl.when(z > 0)
    def _():
        for s in range(2):
            kv_wait(1, p, s)

            @pl.when(z < last)
            def _():
                kv_up(1, s).start()

            kv_side(1, 1, s).start()
            kv_side(1, 0, s).start()

        @pl.when(z < last)
        def _():
            w_up(z, 0).start()

        @pl.when(z < helper)
        def _():
            w_up(z, 1).start()

    def first_plane(s, carry):
        @pl.when(row == 1)
        def _():
            kv_wait(0, across, s)
            kv_forward(0, s).start()

        @pl.when(core == 1)
        def _():
            kv_wait(0, mate, s)

        @pl.when(row == 1)
        def _():
            kv_wait(0, diag, s)

        @pl.when(s == 0)
        def _():
            mark(0, 0, p)

        attend_some(0, 0, p, s, PLANE - 1)
        return carry

    lax.fori_loop(0, 2, first_plane, 0)

    def second_plane(s, carry):
        @pl.when(z < last)
        def _():
            arrive(z + 1, s)

        @pl.when(z > 1)
        def _():
            kv_wait(2, p, s)

            @pl.when(row == 1)
            def _():
                kv_side(2, 1, s).start()

            @pl.when(core == 1)
            def _():
                kv_side(2, 0, s).start()

        @pl.when(z > 0)
        def _():
            kv_wait(1, across, s)
            kv_forward(1, s).start()
            kv_wait(1, mate, s)
            kv_wait(1, diag, s)

            @pl.when(s == 0)
            def _():
                mark(1, 0, PLANE)

            attend(1, 0, PLANE, s, False)

        return carry

    lax.fori_loop(0, 2, second_plane, 0)

    def third_plane(s, carry):
        @pl.when(z > 1)
        def _():
            @pl.when(row == 0)
            def _():
                kv_wait(2, across, s)
                kv_forward(2, s).start()

            @pl.when(core == 0)
            def _():
                kv_wait(2, mate, s)

            @pl.when(row == 0)
            def _():
                kv_wait(2, diag, s)

            @pl.when(s == 0)
            def _():
                mark(2, p, PLANE - p)

            attend_some(2, p, PLANE - p, s, PLANE)

        for n in range(part_heads):
            both = acc[s * part_heads + n]
            attn = both[:, 0:HEAD_SIZE] / both[:, HEAD_SIZE : 2 * HEAD_SIZE]
            abuf[p, s, :, n * HEAD_SIZE : (n + 1) * HEAD_SIZE] = attn.astype(bf)
        a_side(1, s).start()
        a_side(0, s).start()

        @pl.when(z == last)
        def _():
            lend_down(p, s, s).start()

        @pl.when((z == helper) & (s == 0))
        def _():
            arrive(z - 1, 0)

        return carry

    lax.fori_loop(0, 2, third_plane, 0)

    def order(i):
        if i == 0:
            return z
        if i == 1:
            return jnp.where(z < last, z + 1, last - 2)
        if i == 2:
            return jnp.where(z == 0, 2, z - 1)
        return jnp.where(z < 2, last, 0)

    def place(u, pp, part):
        mine = ((u // 2) // per_half) == h
        uu = u % (2 * per_half)

        @pl.when(mine)
        def _():
            keep[uu, pp] = part

        @pl.when(jnp.logical_not(mine))
        def _():
            xsend[uu, pp] = part.astype(bf)
            x_copy(uu, pp).start()

    def attn_of(pp):
        return jnp.concatenate([abuf[pp, 0], abuf[pp, 1]], axis=1)

    def project(j, lo, hi):
        def rows(k, carry):
            pp = target(k)
            both = jnp.concatenate([wbuf[j, 0], wbuf[j, 1]], axis=1)
            part = jnp.dot(attn_of(pp), both, preferred_element_type=f32)
            place(2 * j, pp, part[:, :half])
            place(2 * j + 1, pp, part[:, half:])
            return carry

        lax.fori_loop(lo, hi, rows, 0)

    def project_half(j, s):
        def rows(k, carry):
            pp = target(k)
            part = jnp.dot(attn_of(pp), wbuf[j, s], preferred_element_type=f32)
            place(2 * j + s, pp, part)
            return carry

        lax.fori_loop(0, PLANE, rows, 0)

    def project_lent(lo, hi):
        def rows(k, carry):
            pp = target(k)
            rows_of = jnp.concatenate([lent[pp, 0], lent[pp, 1]], axis=1)
            both = jnp.concatenate([wbuf[0, 0], wbuf[0, 1]], axis=1)
            psend[pp] = jnp.dot(rows_of, both, preferred_element_type=f32).astype(bf)
            give_back(pp).start()
            return carry

        lax.fori_loop(lo, hi, rows, 0)

    def take_back(lo, hi):
        def rows(k, carry):
            pp = target(k)
            copy(
                psend.at[pp], precv.at[pp], p_send.at[pp], p_recv.at[pp], in_plane(mate)
            ).wait_recv()
            for s in range(2):
                cols = slice(s * half, (s + 1) * half)

                @pl.when(h == 0)
                def _():
                    keep[s, pp] = precv[pp, :, cols].astype(f32)

                @pl.when(h > 0)
                def _():
                    copy(
                        precv.at[pp, :, cols], xrecv.at[s, pp], x_send.at[s, pp],
                        x_recv.at[s, pp], (1 - h, c),
                    ).start()

            return carry

        lax.fori_loop(lo, hi, rows, 0)

    def column(u, src):
        return pl.ds(pl.multiple_of(((u // 2) * PLANE + src) * wcols + (u % 2) * half, half), half)

    def finish(j, s):
        @pl.when((j // per_half) == h)
        def _():
            u = (2 * j + s) % (2 * per_half)

            def rows(k, carry):
                pp = target(k)
                x_copy(u, pp).wait_recv()
                done = (keep[u, pp] + xrecv[u, pp].astype(f32)).astype(bf)

                @pl.when(pp == p)
                def _():
                    out_ref[:, column(u, p)] = done

                @pl.when(pp != p)
                def _():
                    rsend[u, pp] = done
                    o_copy(u, pp).start()

                return carry

            lax.fori_loop(0, PLANE, rows, 0)

    def finish_all(j):
        def one(s, carry):
            finish(j, s)
            return carry

        lax.fori_loop(0, 2, one, 0)

    a_wait(mate, 0)
    a_wait(mate, 1)
    project(order(0), 2, PLANE)

    @pl.when(z < last)
    def _():
        project(order(1), 2, PLANE)

        @pl.when(z < helper)
        def _():
            arrive(order(2), 0)

        arrive(order(2), 1)

        @pl.when(z == helper)
        def _():
            w_up(z, 1).start()

        project(order(2), 2, PLANE)

    @pl.when(z == 1)
    def _():
        arrive(order(3), 0)
        arrive(order(3), 1)

    @pl.when(z == helper)
    def _():
        lend_wait(p, 0)
        lend_mate(p, 0, 0).start()

    a_wait(across, 0)
    a_forward(0).start()

    @pl.when(z == last)
    def _():
        lend_down(across, 0, 2).start()
        arrive(order(1), 0)
        arrive(order(1), 1)

    a_wait(across, 1)
    a_forward(1).start()

    @pl.when(z == helper)
    def _():
        lend_wait(p, 1)
        lend_across().start()
        lend_mate(p, 1, 1).start()

    a_wait(diag, 0)
    a_wait(diag, 1)

    @pl.when(z == last)
    def _():
        project(order(1), 0, PLANE)

    project(order(0), 0, 2)

    @pl.when(z < last)
    def _():
        project(order(1), 0, 2)
        project(order(2), 0, 2)

        @pl.when(z != 1)
        def _():
            arrive(order(3), 0)

        project_half(order(3), 0)

        @pl.when(z == helper)
        def _():
            lend_wait(across, 0)
            lend_mate(across, 0, 2).start()

        @pl.when(z != 1)
        def _():
            arrive(order(3), 1)

        @pl.when(z == helper)
        def _():
            lend_wait(mate, 0)
            lend_wait(mate, 1)
            project_lent(2, PLANE)
            lend_wait(across, 1)
            lend_mate(across, 1, 3).start()
            lend_wait(diag, 0)
            lend_wait(diag, 1)
            project_lent(0, 2)

        project_half(order(3), 1)
        for i in range(PLANE):
            finish_all(order(i))

    @pl.when(z == last)
    def _():
        arrive(order(2), 0)
        project_half(order(2), 0)
        finish_all(order(0))
        arrive(order(2), 1)
        project_half(order(2), 1)
        take_back(2, PLANE)
        finish(order(2), 0)
        finish_all(order(1))
        take_back(0, 2)
        finish(order(2), 1)
        finish_all(0)

    def collect(k, carry):
        u = k // PLANE
        src = k % PLANE

        @pl.when(src != p)
        def _():
            copy(
                obuf.at[u, src], obuf.at[u, src], o_send.at[u, src], o_recv.at[u, src],
                in_plane(mate),
            ).wait_recv()
            out_ref[:, column(u, src)] = obuf[u, src]
            o_copy(u, src).wait_send()

        x_copy(u, src).wait_send()
        return carry

    lax.fori_loop(0, 2 * per_half * PLANE, collect, 0)

    for s in range(2):
        a_side(0, s).wait_send()
        a_side(1, s).wait_send()
        a_forward(s).wait_send()

    @pl.when(z == last)
    def _():
        lend_down(p, 0, 0).wait_send()
        lend_down(p, 1, 1).wait_send()
        lend_down(across, 0, 2).wait_send()

    @pl.when(z == helper)
    def _():
        lend_across().wait_send()
        lend_mate(p, 0, 0).wait_send()
        lend_mate(p, 1, 1).wait_send()
        lend_mate(across, 0, 2).wait_send()
        lend_mate(across, 1, 3).wait_send()
        for pp in range(PLANE):
            give_back(pp).wait_send()

    def w_drain(j, carry):
        @pl.when((j <= z) & ((z < helper) | ((z == helper) & (j > 0))))
        def _():
            w_up(j, 0).wait_send()
            w_up(j, 1).wait_send()

        @pl.when((j >= z) & (z > 0))
        def _():
            w_down(j, 0).wait_send()
            w_down(j, 1).wait_send()

        return carry

    lax.fori_loop(0, planes, w_drain, 0)

    for s in range(2):
        @pl.when(z < last)
        def _():
            kv_up(0, s).wait_send()

            @pl.when(z > 0)
            def _():
                kv_up(1, s).wait_send()

        @pl.when(row == 0)
        def _():
            kv_side(0, 1, s).wait_send()

        @pl.when(core == 0)
        def _():
            kv_side(0, 0, s).wait_send()

        @pl.when(row == 1)
        def _():
            kv_forward(0, s).wait_send()

        @pl.when(z > 0)
        def _():
            kv_side(1, 0, s).wait_send()
            kv_side(1, 1, s).wait_send()
            kv_forward(1, s).wait_send()

        @pl.when(z > 1)
        def _():
            @pl.when(row == 1)
            def _():
                kv_side(2, 1, s).wait_send()

            @pl.when(core == 1)
            def _():
                kv_side(2, 0, s).wait_send()

            @pl.when(row == 0)
            def _():
                kv_forward(2, s).wait_send()


def fused_body(n_ctx, n_heads, queries, keys, values, doc_ids, out_weight):
    tok, qcols = queries.shape
    kdim = keys.shape[1]
    groups = kdim // HEAD_SIZE
    krows, wcols = out_weight.shape
    planes = n_ctx // PLANE
    span = QPG * groups
    per_half = planes // n_heads
    docs = jnp.broadcast_to(
        jnp.pad(doc_ids.astype(jnp.bfloat16), (0, kdim - tok))[None, :], (DOC_ROWS, kdim)
    )
    bf, f32 = jnp.bfloat16, jnp.float32
    dma = pltpu.SemaphoreType.DMA
    anywhere = pl.BlockSpec(memory_space=pl.ANY)
    return pl.pallas_call(
        functools.partial(fused_kernel, planes, n_heads, groups, tok, wcols),
        out_shape=jax.ShapeDtypeStruct((tok, per_half * PLANE * wcols), bf),
        in_specs=[pl.BlockSpec(memory_space=pltpu.VMEM), anywhere, anywhere, anywhere, anywhere],
        out_specs=pl.BlockSpec(memory_space=pltpu.VMEM),
        scratch_shapes=[
            pltpu.VMEM((3, PLANE, 2, tok + DOC_ROWS, kdim), bf),
            pltpu.VMEM((3, PLANE, tok, HEAD_SIZE), bf),
            pltpu.VMEM((tok, HEAD_SIZE), bf),
            pltpu.VMEM((planes, 2, krows, wcols // 2), bf),
            pltpu.VMEM((PLANE, 2, tok, krows // 2), bf),
            pltpu.VMEM((PLANE, 2, tok, krows // 2), bf),
            pltpu.VMEM((span, tok, 2 * HEAD_SIZE), f32),
            pltpu.VMEM((span, tok, HEAD_SIZE), f32),
            pltpu.VMEM((2 * per_half, PLANE, tok, wcols // 2), bf),
            pltpu.VMEM((2 * per_half, PLANE, tok, wcols // 2), bf),
            pltpu.VMEM((2 * per_half, PLANE, tok, wcols // 2), f32),
            pltpu.VMEM((2 * per_half, PLANE, tok, wcols // 2), bf),
            pltpu.VMEM((2 * per_half, PLANE, tok, wcols // 2), bf),
            pltpu.VMEM((PLANE, tok, wcols), bf),
            pltpu.VMEM((PLANE, tok, wcols), bf),
            dma((8,)),
            dma((3, PLANE, 2)),
            dma((2, 2)),
            dma((3, 2, 2)),
            dma((3, 2)),
            dma((planes, 2)),
            dma((planes, 2)),
            dma((planes, 2)),
            dma((PLANE, 2)),
            dma((2, 2)),
            dma((2,)),
            dma((2 * per_half, PLANE)),
            dma((2 * per_half, PLANE)),
            dma((2 * per_half, PLANE)),
            dma((2 * per_half, PLANE)),
            dma((PLANE, 2)),
            dma((3,)),
            dma((4,)),
            dma,
            dma((PLANE,)),
            dma((PLANE,)),
        ],
        compiler_params=pltpu.CompilerParams(
            collective_id=0, has_side_effects=True, vmem_limit_bytes=56 * 1024 * 1024
        ),
    )(queries, docs, keys, values, out_weight)


def fits_fused(n_ctx, n_heads, queries, keys, out_weight):
    tokens = queries.shape[0]
    tok = tokens // n_ctx
    reach = min(LOOKBACK_WINDOW, tokens // 2)
    return (
        n_heads == 2
        and n_ctx % PLANE == 0
        and n_ctx // PLANE == 4
        and tok == 2 * HEAD_SIZE
        and reach == 2 * PLANE * tok
        and reach < LOOKBACK_WINDOW
        and keys.shape[1] // n_heads >= tok
        and (out_weight.shape[1] // n_ctx) % 256 == 0
        and keys.shape[1] // n_heads % (2 * HEAD_SIZE) == 0
    )


def passed_along(block, axis, distance):
    devices = range(lax.axis_size(axis))
    route = [(i - distance, i) for i in devices if i - distance in devices]
    return lax.ppermute(block, axis, route)


def body(queries, keys, values, doc_ids, out_weight):
    tok_rows = queries.shape[0]
    groups = keys.shape[1] // HEAD_SIZE
    scale = HEAD_SIZE ** (-0.5)
    q_local = queries.reshape(tok_rows, groups, QPG, HEAD_SIZE)
    here = lax.axis_index("ctx")
    qpos = here * tok_rows + jnp.arange(tok_rows, dtype=jnp.int32)
    reach = LOOKBACK_WINDOW // tok_rows

    def work(state, kblk, vblk, sblk, kstart):
        rowmax, total, accum = state
        scores = (
            jnp.einsum(
                "tgnh,sgh->tgns",
                q_local,
                kblk.reshape(tok_rows, groups, HEAD_SIZE),
                preferred_element_type=jnp.float32,
            )
            * scale
        )
        kpos = kstart + jnp.arange(tok_rows, dtype=jnp.int32)
        vis = (
            (kpos[None, :] <= qpos[:, None])
            & (qpos[:, None] - kpos[None, :] < LOOKBACK_WINDOW)
            & (kpos[None, :] >= 0)
            & (doc_ids[:, None] == sblk[None, :])
        )
        vis = vis[:, None, None, :]
        scores = jnp.where(vis, scores, jnp.float32(-1e30))
        newmax = jnp.maximum(rowmax, jnp.max(scores, axis=-1))
        weights = jnp.where(vis, jnp.exp(scores - newmax[..., None]), jnp.float32(0.0))
        factor = jnp.exp(rowmax - newmax)
        total = total * factor + jnp.sum(weights, axis=-1)
        rounded = weights.astype(jnp.bfloat16)
        contrib = jnp.einsum(
            "tgns,sgh->tgnh",
            rounded,
            vblk.reshape(tok_rows, groups, HEAD_SIZE),
            preferred_element_type=jnp.float32,
        )
        accum = accum * factor[..., None] + contrib
        return (newmax, total, accum)

    def attend(state, kblk, vblk, sblk, kstart):
        return work(state, kblk, vblk, sblk, kstart)

    state = (
        jnp.full((tok_rows, groups, QPG), -1e30, jnp.float32),
        jnp.zeros((tok_rows, groups, QPG), jnp.float32),
        jnp.zeros((tok_rows, groups, QPG, HEAD_SIZE), jnp.float32),
    )
    state = attend(state, keys, values, doc_ids, here * tok_rows)

    def chain_step(depth, carry):
        st, kblk, vblk, sblk = carry
        kblk, vblk, sblk = passed_along((kblk, vblk, sblk), "ctx", 1)
        st = attend(st, kblk, vblk, sblk, (here - depth) * tok_rows)
        return (st, kblk, vblk, sblk)

    state = lax.fori_loop(1, reach + 1, chain_step, (state, keys, values, doc_ids))[0]
    rowmax, total, accum = state
    attn = (
        (accum / total[..., None]).astype(jnp.bfloat16).reshape(tok_rows, groups * QPG * HEAD_SIZE)
    )
    partial_sums = jnp.dot(
        attn,
        lax.all_gather(out_weight, "ctx", axis=1, tiled=True),
        preferred_element_type=jnp.float32,
    )
    return lax.psum_scatter(
        partial_sums.astype(jnp.bfloat16), "heads", scatter_dimension=1, tiled=True
    )


def solution(mesh):
    in_specs = (
        P("ctx", "heads"),
        P("ctx", "heads"),
        P("ctx", "heads"),
        P("ctx"),
        P("heads", "ctx"),
    )
    out_specs = P("ctx", "heads")

    def run(queries, keys, values, doc_ids, out_weight):
        n_ctx, n_heads = mesh.shape["ctx"], mesh.shape["heads"]
        local = body
        if fits_fused(n_ctx, n_heads, queries, keys, out_weight):
            local = functools.partial(fused_body, n_ctx, n_heads)
        return jax.shard_map(
            local, mesh=mesh, in_specs=in_specs, out_specs=out_specs, check_vma=False
        )(queries, keys, values, doc_ids, out_weight)

    return run
```

```python
import functools
import math

import jax
import jax.numpy as jnp
from jax import lax
from jax.experimental import pallas as pl
from jax.experimental.pallas import tpu as pltpu
from jax.sharding import PartitionSpec as P

HEAD_SIZE = 128
LOOKBACK_WINDOW = 4096
QPG = 4


PLANE = 4
DOC_ROWS = 16
MESH = pl.DeviceIdType.MESH


MASKED = 131072.0


def fused_kernel(
    planes, n_heads, groups, tok, wcols,
    q_hbm, docs_hbm, k_hbm, v_hbm, w_hbm, out_ref,
    q_ref, docs_ref, kvbuf, feat, qfeat, wbuf, abuf, lent, acc, rowmax, xsend, xrecv, keep, rsend,
    psend, precv,
    local_sem, kv_recv, kvz_send, kvp_send, kvf_send,
    w_recv, w_right, w_left, a_recv, a_send, a_fwd,
    x_send, x_recv, o_send, o_recv,
    l_recv, l_down, l_mate, l_across, p_send, p_recv, o_own,
):
    h = lax.axis_index("heads")
    c = lax.axis_index("ctx")
    z = c // PLANE
    p = c % PLANE
    core = p % 2
    row = p // 2
    mate = p + 1 - 2 * core
    across = (p + 2) % PLANE
    diag = (mate + 2) % PLANE
    last = planes - 1
    helper = last - 1
    per_half = planes // n_heads
    half = wcols // 2
    pair = groups // 2
    part_heads = QPG * pair
    kcols = pair * HEAD_SIZE
    acols = part_heads * HEAD_SIZE
    bf, f32 = jnp.bfloat16, jnp.float32

    def in_plane(other):
        return (h, z * PLANE + other)

    up = (h, c + PLANE)
    down = (h, c - PLANE)

    def copy(src, dst, send, recv, dev):
        return pltpu.make_async_remote_copy(
            src_ref=src, dst_ref=dst, send_sem=send, recv_sem=recv,
            device_id=dev, device_id_type=MESH,
        )

    def kv_ref(d, who, s):
        return kvbuf.at[d, who, 0] if s == 0 else kvbuf.at[d, who, 1, 0:tok]

    def kv_up(d, s):
        return copy(
            kv_ref(d, p, s), kv_ref(d + 1, p, s), kvz_send.at[d, s], kv_recv.at[d + 1, p, s], up
        )

    def kv_side(d, which, s):
        dev = in_plane(mate if which == 0 else across)
        ref = kv_ref(d, p, s)
        return copy(ref, ref, kvp_send.at[d, which, s], kv_recv.at[d, p, s], dev)

    def kv_forward(d, s):
        ref = kv_ref(d, across, s)
        return copy(ref, ref, kvf_send.at[d, s], kv_recv.at[d, across, s], in_plane(mate))

    def kv_wait(d, who, s):
        ref = kv_ref(d, who, s)
        copy(ref, ref, kvf_send.at[d, s], kv_recv.at[d, who, s], in_plane(mate)).wait_recv()

    def each(s, act):
        for v in range(2):
            pl.when(s == v)(functools.partial(act, v))

    def w_up(j, s):
        ref = wbuf.at[j, s]
        return copy(ref, ref, w_right.at[j, s], w_recv.at[j, s], up)

    def w_down(j, s):
        ref = wbuf.at[j, s]
        return copy(ref, ref, w_left.at[j, s], w_recv.at[j, s], down)

    def arrive(j, s):
        ref = wbuf.at[j, s]
        copy(ref, ref, w_left.at[j, s], w_recv.at[j, s], in_plane(mate)).wait_recv()

        @pl.when((j > z) & (z > 0))
        def _():
            w_down(j, s).start()

        @pl.when((j < z) & ((z < helper) | ((z == helper) & (j > 0))))
        def _():
            w_up(j, s).start()

    def target(k):
        return jnp.where(k == 0, across, jnp.where(k == 1, diag, jnp.where(k == 2, mate, p)))

    def a_part(who, s):
        return abuf.at[who, s]

    def a_side(which, s):
        dev = in_plane(mate if which == 0 else across)
        return copy(a_part(p, s), a_part(p, s), a_send.at[which, s], a_recv.at[p, s], dev)

    def a_forward(s):
        return copy(
            a_part(across, s), a_part(across, s), a_fwd.at[s], a_recv.at[across, s], in_plane(mate)
        )

    def a_wait(who, s):
        copy(
            a_part(who, s), a_part(who, s), a_fwd.at[s], a_recv.at[who, s], in_plane(mate)
        ).wait_recv()

    def lend_down(who, s, slot):
        return copy(a_part(who, s), lent.at[who, s], l_down.at[slot], l_recv.at[who, s], down)

    def lend_mate(who, s, slot):
        ref = lent.at[who, s]
        return copy(ref, ref, l_mate.at[slot], l_recv.at[who, s], in_plane(mate))

    def lend_across():
        ref = lent.at[p, 1]
        return copy(ref, ref, l_across, l_recv.at[p, 1], in_plane(across))

    def lend_wait(who, s):
        ref = lent.at[who, s]
        copy(ref, ref, l_mate.at[0], l_recv.at[who, s], in_plane(mate)).wait_recv()

    def give_back(pp):
        return copy(psend.at[pp], precv.at[pp], p_send.at[pp], p_recv.at[pp], up)

    def x_copy(u, pp):
        return copy(
            xsend.at[u, pp], xrecv.at[u, pp], x_send.at[u, pp], x_recv.at[u, pp], (1 - h, c)
        )

    def column(u, src):
        return pl.ds(pl.multiple_of(((u // 2) * PLANE + src) * wcols + (u % 2) * half, half), half)

    def o_copy(u, pp):
        return copy(
            rsend.at[u, pp], out_ref.at[:, column(u, p)], o_send.at[u, pp], o_recv.at[u, p],
            in_plane(pp),
        )

    def o_local(u):
        return pltpu.make_async_copy(rsend.at[u, p], out_ref.at[:, column(u, p)], o_own.at[u])

    kv_in = []
    for s in range(2):
        cols = slice(s * kcols, (s + 1) * kcols)
        mine = kvbuf.at[0, p, s]
        kv_in.append([
            pltpu.make_async_copy(
                k_hbm.at[:, cols], mine.at[0:tok, 0:kcols], local_sem.at[3 * s]
            ),
            pltpu.make_async_copy(
                v_hbm.at[:, cols], mine.at[0:tok, kcols : 2 * kcols], local_sem.at[3 * s + 1]
            ),
        ])
    docs_in = pltpu.make_async_copy(docs_hbm, docs_ref, local_sem.at[2])
    docs_in.start()
    w_in = [
        pltpu.make_async_copy(
            w_hbm.at[:, s * half : (s + 1) * half], wbuf.at[z, s], local_sem.at[6 + s]
        )
        for s in range(2)
    ]
    for s in range(2):
        for one in kv_in[s]:
            one.start()
    q_in = pltpu.make_async_copy(q_hbm, q_ref, local_sem.at[8])
    q_in.start()
    w_in[0].start()
    w_in[1].start()

    barrier = pltpu.get_barrier_semaphore()
    for dev in (in_plane(mate), in_plane(across), in_plane(diag), (1 - h, c)):
        pl.semaphore_signal(barrier, inc=1, device_id=dev, device_id_type=MESH)

    @pl.when(z < last)
    def _():
        pl.semaphore_signal(barrier, inc=1, device_id=up, device_id_type=MESH)

    @pl.when(z > 0)
    def _():
        pl.semaphore_signal(barrier, inc=1, device_id=down, device_id_type=MESH)

    docs_in.wait()
    kvbuf[0, p, 0, tok : tok + DOC_ROWS, 0:tok] = jnp.broadcast_to(
        docs_ref[...].astype(f32), (DOC_ROWS, tok)
    ).astype(bf)
    pl.semaphore_wait(barrier, 4 + jnp.minimum(z, 1) + jnp.minimum(last - z, 1))

    for s in range(2):
        for one in kv_in[s]:
            one.wait()

        @pl.when(z < last)
        def _():
            kv_up(0, s).start()

        @pl.when(row == 0)
        def _():
            kv_side(0, 1, s).start()

        @pl.when(core == 0)
        def _():
            kv_side(0, 0, s).start()

    for s in range(2):
        w_in[s].wait()

        @pl.when(z > 0)
        def _():
            w_down(z, s).start()

        @pl.when(z == 0)
        def _():
            w_up(z, s).start()

    factor = HEAD_SIZE ** (-0.5) * math.log2(math.e)

    def same_lane(d, who):
        docs = kvbuf[d, who, 0, tok : tok + DOC_ROWS, 0:tok].astype(f32)[0:1, :]
        column = jnp.broadcast_to(docs, (HEAD_SIZE, tok)).T
        return column == lax.broadcasted_iota(jnp.int32, (tok, HEAD_SIZE), 1).astype(f32)

    def mark(d, lo, count):
        def one(k, carry):
            hit = same_lane(d, lo + k)
            feat[d, lo + k] = jnp.where(hit, jnp.float32(1.0), jnp.float32(0.0)).astype(bf)
            return carry

        lax.fori_loop(0, count, one, 0)

    def attend(d, lo, blocks, s, first):
        ones = jnp.ones((tok, HEAD_SIZE), bf)
        lanes = 2 * HEAD_SIZE
        heads, keys, vals = [], [], []
        for u in range(pair):
            kc = slice(u * HEAD_SIZE, (u + 1) * HEAD_SIZE)
            vc = slice(kcols + u * HEAD_SIZE, kcols + (u + 1) * HEAD_SIZE)
            kb = [
                jnp.concatenate([kvbuf[d, lo + b, s, 0:tok, kc], feat[d, lo + b]], axis=1)
                for b in range(blocks)
            ]
            vb = [
                jnp.concatenate([kvbuf[d, lo + b, s, 0:tok, vc], ones], axis=1)
                for b in range(blocks)
            ]
            for n in range(QPG):
                heads.append(s * part_heads + u * QPG + n)
                keys.append(kb)
                vals.append(vb)
        keys = [jnp.concatenate(kb, axis=0) if blocks > 1 else kb[0] for kb in keys]
        vals = [jnp.concatenate(vb, axis=0) if blocks > 1 else vb[0] for vb in vals]
        if not first:
            olds = [rowmax[head] for head in heads]
            accs = [acc[head] for head in heads]
        done = []
        for n, head in enumerate(heads):
            cols = pl.ds(pl.multiple_of(head * HEAD_SIZE, HEAD_SIZE), HEAD_SIZE)
            qs = jnp.concatenate([q_ref[:, cols], qfeat[...]], axis=1)
            scores = lax.dot_general(
                qs, keys[n], (((1,), (1,)), ((), ())), preferred_element_type=f32
            )
            if first:
                qpos = lax.broadcasted_iota(jnp.int32, (tok, tok), 0)
                kpos = lax.broadcasted_iota(jnp.int32, (tok, tok), 1)
                scores = jnp.where(kpos <= qpos, scores, jnp.float32(-1e30))
            top = functools.reduce(
                jnp.maximum,
                [scores[:, i : i + HEAD_SIZE] for i in range(0, blocks * tok, HEAD_SIZE)],
            )
            top = jnp.max(top, axis=1, keepdims=True)
            if not first:
                top = jnp.maximum(top, olds[n][:, 0:1])
            weights = jnp.exp2((scores - top) * factor).astype(bf)
            both = jnp.dot(weights, vals[n], preferred_element_type=f32)
            if not first:
                shrink = jnp.exp2((olds[n] - top) * factor)
                both = accs[n] * jnp.concatenate([shrink, shrink], axis=1) + both
            done.append((jnp.broadcast_to(top, (tok, HEAD_SIZE)), both))
        for head, (top, both) in zip(heads, done):
            rowmax[head] = top
            acc[head] = both

    def attend_some(d, lo, count, s, most):
        for blocks in range(1, most + 1):

            @pl.when(count == blocks)
            def _():
                attend(d, lo, blocks, s, False)

    qfeat[...] = jnp.where(same_lane(0, p), jnp.float32(0.0), jnp.float32(-MASKED)).astype(bf)
    mark(0, p, 1)

    def own_half(s, carry):
        attend(0, p, 1, s, True)
        return carry

    q_in.wait()
    lax.fori_loop(0, 2, own_half, 0)

    @pl.when(z > 0)
    def _():
        for s in range(2):
            kv_wait(1, p, s)

            @pl.when(z < last)
            def _():
                kv_up(1, s).start()

            kv_side(1, 1, s).start()
            kv_side(1, 0, s).start()

        @pl.when(z < last)
        def _():
            w_up(z, 0).start()

        @pl.when(z < helper)
        def _():
            w_up(z, 1).start()

    def first_plane(s, carry):
        def settle(v):
            @pl.when(row == 1)
            def _():
                kv_wait(0, across, v)
                kv_forward(0, v).start()

            @pl.when(core == 1)
            def _():
                kv_wait(0, mate, v)

            @pl.when(row == 1)
            def _():
                kv_wait(0, diag, v)

        each(s, settle)

        @pl.when(s == 0)
        def _():
            mark(0, 0, p)

        attend_some(0, 0, p, s, PLANE - 1)
        return carry

    lax.fori_loop(0, 2, first_plane, 0)

    def second_plane(s, carry):
        @pl.when(z < last)
        def _():
            arrive(z + 1, s)

        def pass_on(v):
            kv_wait(2, p, v)

            @pl.when(row == 1)
            def _():
                kv_side(2, 1, v).start()

            @pl.when(core == 1)
            def _():
                kv_side(2, 0, v).start()

        def settle(v):
            kv_wait(1, across, v)
            kv_forward(1, v).start()
            kv_wait(1, mate, v)
            kv_wait(1, diag, v)

        @pl.when(z > 1)
        def _():
            each(s, pass_on)

        @pl.when(z > 0)
        def _():
            each(s, settle)

            @pl.when(s == 0)
            def _():
                mark(1, 0, PLANE)

            attend(1, 0, PLANE, s, False)

        return carry

    lax.fori_loop(0, 2, second_plane, 0)

    def third_plane(s, carry):
        def settle(v):
            @pl.when(row == 0)
            def _():
                kv_wait(2, across, v)
                kv_forward(2, v).start()

            @pl.when(core == 0)
            def _():
                kv_wait(2, mate, v)

            @pl.when(row == 0)
            def _():
                kv_wait(2, diag, v)

        @pl.when(z > 1)
        def _():
            each(s, settle)

            @pl.when(s == 0)
            def _():
                mark(2, p, PLANE - p)

            attend_some(2, p, PLANE - p, s, PLANE)

        for n in range(part_heads):
            both = acc[s * part_heads + n]
            attn = both[:, 0:HEAD_SIZE] / both[:, HEAD_SIZE : 2 * HEAD_SIZE]
            abuf[p, s, :, n * HEAD_SIZE : (n + 1) * HEAD_SIZE] = attn.astype(bf)
        a_side(1, s).start()
        a_side(0, s).start()

        @pl.when(z == last)
        def _():
            lend_down(p, s, s).start()

        @pl.when((z == helper) & (s == 0))
        def _():
            arrive(z - 1, 0)

        return carry

    lax.fori_loop(0, 2, third_plane, 0)

    def order(i):
        if i == 0:
            return z
        if i == 1:
            return jnp.where(z < last, z + 1, last - 2)
        if i == 2:
            return jnp.where(z == 0, 2, z - 1)
        return jnp.where(z < 2, last, 0)

    def place(u, pp, part):
        mine = ((u // 2) // per_half) == h
        uu = u % (2 * per_half)

        @pl.when(mine)
        def _():
            keep[uu, pp] = part

        @pl.when(jnp.logical_not(mine))
        def _():
            xsend[uu, pp] = part.astype(bf)
            x_copy(uu, pp).start()

    def attn_of(pp):
        return jnp.concatenate([abuf[pp, 0], abuf[pp, 1]], axis=1)

    def project(j, lo, hi):
        def rows(k, carry):
            pp = target(k)
            both = jnp.concatenate([wbuf[j, 0], wbuf[j, 1]], axis=1)
            part = jnp.dot(attn_of(pp), both, preferred_element_type=f32)
            place(2 * j, pp, part[:, :half])
            place(2 * j + 1, pp, part[:, half:])
            return carry

        lax.fori_loop(lo, hi, rows, 0)

    def project_half(j, s):
        def rows(k, carry):
            pp = target(k)
            part = jnp.dot(attn_of(pp), wbuf[j, s], preferred_element_type=f32)
            place(2 * j + s, pp, part)
            return carry

        lax.fori_loop(0, PLANE, rows, 0)

    def project_lent(lo, hi):
        def rows(k, carry):
            pp = target(k)
            rows_of = jnp.concatenate([lent[pp, 0], lent[pp, 1]], axis=1)
            both = jnp.concatenate([wbuf[0, 0], wbuf[0, 1]], axis=1)
            psend[pp] = jnp.dot(rows_of, both, preferred_element_type=f32).astype(bf)
            give_back(pp).start()
            return carry

        lax.fori_loop(lo, hi, rows, 0)

    def take_back(lo, hi):
        def rows(k, carry):
            pp = target(k)
            copy(
                psend.at[pp], precv.at[pp], p_send.at[pp], p_recv.at[pp], in_plane(mate)
            ).wait_recv()
            for s in range(2):
                cols = slice(s * half, (s + 1) * half)

                @pl.when(h == 0)
                def _():
                    keep[s, pp] = precv[pp, :, cols].astype(f32)

                @pl.when(h > 0)
                def _():
                    copy(
                        precv.at[pp, :, cols], xrecv.at[s, pp], x_send.at[s, pp],
                        x_recv.at[s, pp], (1 - h, c),
                    ).start()

            return carry

        lax.fori_loop(lo, hi, rows, 0)

    def settle_rows(u, lo, hi):
        def rows(k, carry):
            pp = target(k)
            x_copy(u, pp).wait_recv()
            rsend[u, pp] = (keep[u, pp] + xrecv[u, pp].astype(f32)).astype(bf)

            @pl.when(pp == p)
            def _():
                o_local(u).start()

            @pl.when(pp != p)
            def _():
                o_copy(u, pp).start()

            return carry

        lax.fori_loop(lo, hi, rows, 0)

    def finish(j, s):
        @pl.when((j // per_half) == h)
        def _():
            settle_rows((2 * j + s) % (2 * per_half), 0, PLANE)

    def finish_rows(lo, hi):
        @pl.when(h == 0)
        def _():
            def one(k, carry):
                def both(s, inner):
                    settle_rows(s, k, k + 1)
                    return inner

                lax.fori_loop(0, 2, both, 0)
                return carry

            lax.fori_loop(lo, hi, one, 0)

    def finish_all(j):
        def one(s, carry):
            finish(j, s)
            return carry

        lax.fori_loop(0, 2, one, 0)

    a_wait(mate, 0)
    a_wait(mate, 1)
    project(order(0), 2, PLANE)

    @pl.when(z < last)
    def _():
        project(order(1), 2, PLANE)

        @pl.when(z < helper)
        def _():
            arrive(order(2), 0)

        arrive(order(2), 1)

        @pl.when(z == helper)
        def _():
            w_up(z, 1).start()

        project(order(2), 2, PLANE)

    @pl.when(z == 1)
    def _():
        arrive(order(3), 0)
        arrive(order(3), 1)

    @pl.when(z == helper)
    def _():
        lend_wait(p, 0)
        lend_mate(p, 0, 0).start()

    a_wait(across, 0)
    a_forward(0).start()

    @pl.when(z == last)
    def _():
        lend_down(across, 0, 2).start()
        arrive(order(1), 0)
        arrive(order(1), 1)

    a_wait(across, 1)
    a_forward(1).start()

    @pl.when(z == helper)
    def _():
        lend_wait(p, 1)
        lend_across().start()
        lend_mate(p, 1, 1).start()

    a_wait(diag, 0)
    a_wait(diag, 1)

    @pl.when(z == last)
    def _():
        project(order(1), 0, PLANE)

    project(order(0), 0, 2)

    @pl.when(z < last)
    def _():
        project(order(1), 0, 2)
        project(order(2), 0, 2)

        @pl.when(z != 1)
        def _():
            arrive(order(3), 0)

        project_half(order(3), 0)

        for i in range(PLANE - 1):
            finish_all(order(i))

        @pl.when(z == helper)
        def _():
            lend_wait(across, 0)
            lend_mate(across, 0, 2).start()

        @pl.when(z != 1)
        def _():
            arrive(order(3), 1)

        @pl.when(z == helper)
        def _():
            lend_wait(across, 1)
            lend_mate(across, 1, 3).start()
            project_lent(0, 1)
            lend_wait(diag, 0)
            lend_wait(diag, 1)
            lend_wait(mate, 0)
            lend_wait(mate, 1)
            project_lent(1, PLANE)

        project_half(order(3), 1)
        finish_all(order(3))

    @pl.when(z == last)
    def _():
        arrive(order(2), 0)
        project_half(order(2), 0)
        finish_all(order(0))
        arrive(order(2), 1)
        project_half(order(2), 1)
        finish_all(order(1))
        take_back(0, 2)
        finish_all(order(2))
        finish_rows(0, 2)
        take_back(2, PLANE)
        finish_rows(2, PLANE)

    def collect(k, carry):
        u = k // PLANE
        src = k % PLANE

        @pl.when(src != p)
        def _():
            copy(
                rsend.at[u, src], out_ref.at[:, column(u, src)], o_send.at[u, src],
                o_recv.at[u, src], in_plane(mate),
            ).wait_recv()
            o_copy(u, src).wait_send()

        @pl.when(src == p)
        def _():
            o_local(u).wait()

        x_copy(u, src).wait_send()
        return carry

    lax.fori_loop(0, 2 * per_half * PLANE, collect, 0)

    for s in range(2):
        a_side(0, s).wait_send()
        a_side(1, s).wait_send()
        a_forward(s).wait_send()

    @pl.when(z == last)
    def _():
        lend_down(p, 0, 0).wait_send()
        lend_down(p, 1, 1).wait_send()
        lend_down(across, 0, 2).wait_send()

    @pl.when(z == helper)
    def _():
        lend_across().wait_send()
        lend_mate(p, 0, 0).wait_send()
        lend_mate(p, 1, 1).wait_send()
        lend_mate(across, 0, 2).wait_send()
        lend_mate(across, 1, 3).wait_send()
        for pp in range(PLANE):
            give_back(pp).wait_send()

    def w_drain(j, carry):
        @pl.when((j <= z) & ((z < helper) | ((z == helper) & (j > 0))))
        def _():
            w_up(j, 0).wait_send()
            w_up(j, 1).wait_send()

        @pl.when((j >= z) & (z > 0))
        def _():
            w_down(j, 0).wait_send()
            w_down(j, 1).wait_send()

        return carry

    lax.fori_loop(0, planes, w_drain, 0)

    for s in range(2):
        @pl.when(z < last)
        def _():
            kv_up(0, s).wait_send()

            @pl.when(z > 0)
            def _():
                kv_up(1, s).wait_send()

        @pl.when(row == 0)
        def _():
            kv_side(0, 1, s).wait_send()

        @pl.when(core == 0)
        def _():
            kv_side(0, 0, s).wait_send()

        @pl.when(row == 1)
        def _():
            kv_forward(0, s).wait_send()

        @pl.when(z > 0)
        def _():
            kv_side(1, 0, s).wait_send()
            kv_side(1, 1, s).wait_send()
            kv_forward(1, s).wait_send()

        @pl.when(z > 1)
        def _():
            @pl.when(row == 1)
            def _():
                kv_side(2, 1, s).wait_send()

            @pl.when(core == 1)
            def _():
                kv_side(2, 0, s).wait_send()

            @pl.when(row == 0)
            def _():
                kv_forward(2, s).wait_send()


def fused_body(n_ctx, n_heads, queries, keys, values, doc_ids, out_weight):
    tok, qcols = queries.shape
    kdim = keys.shape[1]
    groups = kdim // HEAD_SIZE
    krows, wcols = out_weight.shape
    planes = n_ctx // PLANE
    span = QPG * groups
    per_half = planes // n_heads
    bf, f32 = jnp.bfloat16, jnp.float32
    dma = pltpu.SemaphoreType.DMA
    hbm = functools.partial(pltpu.with_memory_space_constraint, memory_space=pltpu.HBM)
    anywhere = pl.BlockSpec(memory_space=pl.ANY)
    return pl.pallas_call(
        functools.partial(fused_kernel, planes, n_heads, groups, tok, wcols),
        out_shape=jax.ShapeDtypeStruct((tok, per_half * PLANE * wcols), bf),
        in_specs=[pl.BlockSpec(memory_space=pltpu.HBM)] * 5,
        out_specs=anywhere,
        scratch_shapes=[
            pltpu.VMEM((tok, qcols), bf),
            pltpu.VMEM((1, tok), jnp.int32),
            pltpu.VMEM((3, PLANE, 2, tok + DOC_ROWS, kdim), bf),
            pltpu.VMEM((3, PLANE, tok, HEAD_SIZE), bf),
            pltpu.VMEM((tok, HEAD_SIZE), bf),
            pltpu.VMEM((planes, 2, krows, wcols // 2), bf),
            pltpu.VMEM((PLANE, 2, tok, krows // 2), bf),
            pltpu.VMEM((PLANE, 2, tok, krows // 2), bf),
            pltpu.VMEM((span, tok, 2 * HEAD_SIZE), f32),
            pltpu.VMEM((span, tok, HEAD_SIZE), f32),
            pltpu.VMEM((2 * per_half, PLANE, tok, wcols // 2), bf),
            pltpu.VMEM((2 * per_half, PLANE, tok, wcols // 2), bf),
            pltpu.VMEM((2 * per_half, PLANE, tok, wcols // 2), f32),
            pltpu.VMEM((2 * per_half, PLANE, tok, wcols // 2), bf),
            pltpu.VMEM((PLANE, tok, wcols), bf),
            pltpu.VMEM((PLANE, tok, wcols), bf),
            dma((9,)),
            dma((3, PLANE, 2)),
            dma((2, 2)),
            dma((3, 2, 2)),
            dma((3, 2)),
            dma((planes, 2)),
            dma((planes, 2)),
            dma((planes, 2)),
            dma((PLANE, 2)),
            dma((2, 2)),
            dma((2,)),
            dma((2 * per_half, PLANE)),
            dma((2 * per_half, PLANE)),
            dma((2 * per_half, PLANE)),
            dma((2 * per_half, PLANE)),
            dma((PLANE, 2)),
            dma((3,)),
            dma((4,)),
            dma,
            dma((PLANE,)),
            dma((PLANE,)),
            dma((2 * per_half,)),
        ],
        compiler_params=pltpu.CompilerParams(
            collective_id=0, has_side_effects=True, vmem_limit_bytes=44 * 1024 * 1024
        ),
    )(hbm(queries), hbm(doc_ids[None, :]), hbm(keys), hbm(values), hbm(out_weight))


def fits_fused(n_ctx, n_heads, queries, keys, out_weight):
    tokens = queries.shape[0]
    tok = tokens // n_ctx
    reach = min(LOOKBACK_WINDOW, tokens // 2)
    return (
        n_heads == 2
        and n_ctx % PLANE == 0
        and n_ctx // PLANE == 4
        and tok == 2 * HEAD_SIZE
        and reach == 2 * PLANE * tok
        and reach < LOOKBACK_WINDOW
        and keys.shape[1] // n_heads >= tok
        and (out_weight.shape[1] // n_ctx) % 256 == 0
        and keys.shape[1] // n_heads % (2 * HEAD_SIZE) == 0
    )


def passed_along(block, axis, distance):
    devices = range(lax.axis_size(axis))
    route = [(i - distance, i) for i in devices if i - distance in devices]
    return lax.ppermute(block, axis, route)


def body(queries, keys, values, doc_ids, out_weight):
    tok_rows = queries.shape[0]
    groups = keys.shape[1] // HEAD_SIZE
    scale = HEAD_SIZE ** (-0.5)
    q_local = queries.reshape(tok_rows, groups, QPG, HEAD_SIZE)
    here = lax.axis_index("ctx")
    qpos = here * tok_rows + jnp.arange(tok_rows, dtype=jnp.int32)
    reach = LOOKBACK_WINDOW // tok_rows

    def work(state, kblk, vblk, sblk, kstart):
        rowmax, total, accum = state
        scores = (
            jnp.einsum(
                "tgnh,sgh->tgns",
                q_local,
                kblk.reshape(tok_rows, groups, HEAD_SIZE),
                preferred_element_type=jnp.float32,
            )
            * scale
        )
        kpos = kstart + jnp.arange(tok_rows, dtype=jnp.int32)
        vis = (
            (kpos[None, :] <= qpos[:, None])
            & (qpos[:, None] - kpos[None, :] < LOOKBACK_WINDOW)
            & (kpos[None, :] >= 0)
            & (doc_ids[:, None] == sblk[None, :])
        )
        vis = vis[:, None, None, :]
        scores = jnp.where(vis, scores, jnp.float32(-1e30))
        newmax = jnp.maximum(rowmax, jnp.max(scores, axis=-1))
        weights = jnp.where(vis, jnp.exp(scores - newmax[..., None]), jnp.float32(0.0))
        factor = jnp.exp(rowmax - newmax)
        total = total * factor + jnp.sum(weights, axis=-1)
        rounded = weights.astype(jnp.bfloat16)
        contrib = jnp.einsum(
            "tgns,sgh->tgnh",
            rounded,
            vblk.reshape(tok_rows, groups, HEAD_SIZE),
            preferred_element_type=jnp.float32,
        )
        accum = accum * factor[..., None] + contrib
        return (newmax, total, accum)

    def attend(state, kblk, vblk, sblk, kstart):
        return work(state, kblk, vblk, sblk, kstart)

    state = (
        jnp.full((tok_rows, groups, QPG), -1e30, jnp.float32),
        jnp.zeros((tok_rows, groups, QPG), jnp.float32),
        jnp.zeros((tok_rows, groups, QPG, HEAD_SIZE), jnp.float32),
    )
    state = attend(state, keys, values, doc_ids, here * tok_rows)

    def chain_step(depth, carry):
        st, kblk, vblk, sblk = carry
        kblk, vblk, sblk = passed_along((kblk, vblk, sblk), "ctx", 1)
        st = attend(st, kblk, vblk, sblk, (here - depth) * tok_rows)
        return (st, kblk, vblk, sblk)

    state = lax.fori_loop(1, reach + 1, chain_step, (state, keys, values, doc_ids))[0]
    rowmax, total, accum = state
    attn = (
        (accum / total[..., None]).astype(jnp.bfloat16).reshape(tok_rows, groups * QPG * HEAD_SIZE)
    )
    partial_sums = jnp.dot(
        attn,
        lax.all_gather(out_weight, "ctx", axis=1, tiled=True),
        preferred_element_type=jnp.float32,
    )
    return lax.psum_scatter(
        partial_sums.astype(jnp.bfloat16), "heads", scatter_dimension=1, tiled=True
    )


def solution(mesh):
    in_specs = (
        P("ctx", "heads"),
        P("ctx", "heads"),
        P("ctx", "heads"),
        P("ctx"),
        P("heads", "ctx"),
    )
    out_specs = P("ctx", "heads")

    def run(queries, keys, values, doc_ids, out_weight):
        n_ctx, n_heads = mesh.shape["ctx"], mesh.shape["heads"]
        local = body
        if fits_fused(n_ctx, n_heads, queries, keys, out_weight):
            local = functools.partial(fused_body, n_ctx, n_heads)
        return jax.shard_map(
            local, mesh=mesh, in_specs=in_specs, out_specs=out_specs, check_vma=False
        )(queries, keys, values, doc_ids, out_weight)

    return run
```

```python
import functools
import math

import jax
import jax.numpy as jnp
from jax import lax
from jax.experimental import pallas as pl
from jax.experimental.pallas import tpu as pltpu
from jax.sharding import PartitionSpec as P

HEAD_SIZE = 128
LOOKBACK_WINDOW = 4096
QPG = 4


PLANE = 4
DOC_ROWS = 16
MESH = pl.DeviceIdType.MESH


MASKED = 131072.0


def fused_kernel(
    planes, n_heads, groups, tok, wcols,
    q_hbm, docs_hbm, k_hbm, v_hbm, w_hbm, out_ref,
    q_ref, docs_ref, kvbuf, feat, qfeat, wbuf, abuf, lent, acc, rowmax, xsend, xrecv, keep, rsend,
    psend, precv,
    local_sem, kv_recv, kvz_send, kvp_send, kvf_send,
    w_recv, w_right, w_left, a_recv, a_send, a_fwd,
    x_send, x_recv, o_send, o_recv,
    l_recv, l_down, l_mate, l_across, p_send, p_recv, o_own,
):
    h = lax.axis_index("heads")
    c = lax.axis_index("ctx")
    z = c // PLANE
    p = c % PLANE
    core = p % 2
    row = p // 2
    mate = p + 1 - 2 * core
    across = (p + 2) % PLANE
    diag = (mate + 2) % PLANE
    last = planes - 1
    helper = last - 1
    per_half = planes // n_heads
    half = wcols // 2
    pair = groups // 2
    part_heads = QPG * pair
    kcols = pair * HEAD_SIZE
    acols = part_heads * HEAD_SIZE
    bf, f32 = jnp.bfloat16, jnp.float32

    def in_plane(other):
        return (h, z * PLANE + other)

    up = (h, c + PLANE)
    down = (h, c - PLANE)

    def copy(src, dst, send, recv, dev):
        return pltpu.make_async_remote_copy(
            src_ref=src, dst_ref=dst, send_sem=send, recv_sem=recv,
            device_id=dev, device_id_type=MESH,
        )

    def kv_ref(d, who, s):
        return kvbuf.at[d, who, 0] if s == 0 else kvbuf.at[d, who, 1, 0:tok]

    def kv_up(d, s):
        return copy(
            kv_ref(d, p, s), kv_ref(d + 1, p, s), kvz_send.at[d, s], kv_recv.at[d + 1, p, s], up
        )

    def kv_side(d, which, s):
        dev = in_plane(mate if which == 0 else across)
        ref = kv_ref(d, p, s)
        return copy(ref, ref, kvp_send.at[d, which, s], kv_recv.at[d, p, s], dev)

    def kv_forward(d, s):
        ref = kv_ref(d, across, s)
        return copy(ref, ref, kvf_send.at[d, s], kv_recv.at[d, across, s], in_plane(mate))

    def kv_wait(d, who, s):
        ref = kv_ref(d, who, s)
        copy(ref, ref, kvf_send.at[d, s], kv_recv.at[d, who, s], in_plane(mate)).wait_recv()

    def each(s, act):
        for v in range(2):
            pl.when(s == v)(functools.partial(act, v))

    def w_up(j, s):
        ref = wbuf.at[j, s]
        return copy(ref, ref, w_right.at[j, s], w_recv.at[j, s], up)

    def w_down(j, s):
        ref = wbuf.at[j, s]
        return copy(ref, ref, w_left.at[j, s], w_recv.at[j, s], down)

    def arrive(j, s):
        ref = wbuf.at[j, s]
        copy(ref, ref, w_left.at[j, s], w_recv.at[j, s], in_plane(mate)).wait_recv()

        @pl.when((j > z) & (z > 0))
        def _():
            w_down(j, s).start()

        @pl.when((j < z) & ((z < helper) | ((z == helper) & (j > 0))))
        def _():
            w_up(j, s).start()

    def target(k):
        return jnp.where(k == 0, across, jnp.where(k == 1, diag, jnp.where(k == 2, mate, p)))

    def a_part(who, s):
        return abuf.at[who, s]

    def a_side(which, s):
        dev = in_plane(mate if which == 0 else across)
        return copy(a_part(p, s), a_part(p, s), a_send.at[which, s], a_recv.at[p, s], dev)

    def a_forward(s):
        return copy(
            a_part(across, s), a_part(across, s), a_fwd.at[s], a_recv.at[across, s], in_plane(mate)
        )

    def a_wait(who, s):
        copy(
            a_part(who, s), a_part(who, s), a_fwd.at[s], a_recv.at[who, s], in_plane(mate)
        ).wait_recv()

    def lend_down(who, s, slot):
        return copy(a_part(who, s), lent.at[who, s], l_down.at[slot], l_recv.at[who, s], down)

    def lend_mate(who, s, slot):
        ref = lent.at[who, s]
        return copy(ref, ref, l_mate.at[slot], l_recv.at[who, s], in_plane(mate))

    def lend_across():
        ref = lent.at[p, 1]
        return copy(ref, ref, l_across, l_recv.at[p, 1], in_plane(across))

    def lend_wait(who, s):
        ref = lent.at[who, s]
        copy(ref, ref, l_mate.at[0], l_recv.at[who, s], in_plane(mate)).wait_recv()

    def give_back(pp):
        return copy(psend.at[pp], precv.at[pp], p_send.at[pp], p_recv.at[pp], up)

    def x_copy(u, pp):
        return copy(
            xsend.at[u, pp], xrecv.at[u, pp], x_send.at[u, pp], x_recv.at[u, pp], (1 - h, c)
        )

    def column(u, src):
        return pl.ds(pl.multiple_of(((u // 2) * PLANE + src) * wcols + (u % 2) * half, half), half)

    def o_copy(u, pp):
        return copy(
            rsend.at[u, pp], out_ref.at[:, column(u, p)], o_send.at[u, pp], o_recv.at[u, p],
            in_plane(pp),
        )

    def o_local(u):
        return pltpu.make_async_copy(rsend.at[u, p], out_ref.at[:, column(u, p)], o_own.at[u])

    kv_in = []
    for s in range(2):
        cols = slice(s * kcols, (s + 1) * kcols)
        mine = kvbuf.at[0, p, s]
        kv_in.append([
            pltpu.make_async_copy(
                k_hbm.at[:, cols], mine.at[0:tok, 0:kcols], local_sem.at[3 * s]
            ),
            pltpu.make_async_copy(
                v_hbm.at[:, cols], mine.at[0:tok, kcols : 2 * kcols], local_sem.at[3 * s + 1]
            ),
        ])
    docs_in = pltpu.make_async_copy(docs_hbm, docs_ref, local_sem.at[2])
    docs_in.start()
    w_in = [
        pltpu.make_async_copy(
            w_hbm.at[:, s * half : (s + 1) * half], wbuf.at[z, s], local_sem.at[6 + s]
        )
        for s in range(2)
    ]
    for s in range(2):
        for one in kv_in[s]:
            one.start()
    q_in = pltpu.make_async_copy(q_hbm, q_ref, local_sem.at[8])
    q_in.start()
    w_in[0].start()
    w_in[1].start()

    barrier = pltpu.get_barrier_semaphore()
    for dev in (in_plane(mate), in_plane(across), in_plane(diag), (1 - h, c)):
        pl.semaphore_signal(barrier, inc=1, device_id=dev, device_id_type=MESH)

    @pl.when(z < last)
    def _():
        pl.semaphore_signal(barrier, inc=1, device_id=up, device_id_type=MESH)

    @pl.when(z > 0)
    def _():
        pl.semaphore_signal(barrier, inc=1, device_id=down, device_id_type=MESH)

    docs_in.wait()
    kvbuf[0, p, 0, tok : tok + DOC_ROWS, 0:tok] = jnp.broadcast_to(
        docs_ref[...].astype(f32), (DOC_ROWS, tok)
    ).astype(bf)
    pl.semaphore_wait(barrier, 4 + jnp.minimum(z, 1) + jnp.minimum(last - z, 1))

    for s in range(2):
        for one in kv_in[s]:
            one.wait()

        @pl.when(z < last)
        def _():
            kv_up(0, s).start()

        @pl.when(row == 0)
        def _():
            kv_side(0, 1, s).start()

        @pl.when(core == 0)
        def _():
            kv_side(0, 0, s).start()

    for s in range(2):
        w_in[s].wait()

        @pl.when(z > 0)
        def _():
            w_down(z, s).start()

        @pl.when(z == 0)
        def _():
            w_up(z, s).start()

    factor = HEAD_SIZE ** (-0.5) * math.log2(math.e)

    def same_lane(d, who):
        docs = kvbuf[d, who, 0, tok : tok + DOC_ROWS, 0:tok].astype(f32)[0:1, :]
        column = jnp.broadcast_to(docs, (HEAD_SIZE, tok)).T
        return column == lax.broadcasted_iota(jnp.int32, (tok, HEAD_SIZE), 1).astype(f32)

    def mark(d, lo, count):
        def one(k, carry):
            hit = same_lane(d, lo + k)
            feat[d, lo + k] = jnp.where(hit, jnp.float32(1.0), jnp.float32(0.0)).astype(bf)
            return carry

        lax.fori_loop(0, count, one, 0)

    def attend(d, lo, blocks, s, first):
        ones = jnp.ones((tok, HEAD_SIZE), bf)
        lanes = 2 * HEAD_SIZE
        heads, keys, vals = [], [], []
        for u in range(pair):
            kc = slice(u * HEAD_SIZE, (u + 1) * HEAD_SIZE)
            vc = slice(kcols + u * HEAD_SIZE, kcols + (u + 1) * HEAD_SIZE)
            kb = [
                jnp.concatenate([kvbuf[d, lo + b, s, 0:tok, kc], feat[d, lo + b]], axis=1)
                for b in range(blocks)
            ]
            vb = [
                jnp.concatenate([kvbuf[d, lo + b, s, 0:tok, vc], ones], axis=1)
                for b in range(blocks)
            ]
            for n in range(QPG):
                heads.append(s * part_heads + u * QPG + n)
                keys.append(kb)
                vals.append(vb)
        keys = [jnp.concatenate(kb, axis=0) if blocks > 1 else kb[0] for kb in keys]
        vals = [jnp.concatenate(vb, axis=0) if blocks > 1 else vb[0] for vb in vals]
        if not first:
            olds = [rowmax[head] for head in heads]
            accs = [acc[head] for head in heads]
        done = []
        for n, head in enumerate(heads):
            cols = pl.ds(pl.multiple_of(head * HEAD_SIZE, HEAD_SIZE), HEAD_SIZE)
            qs = jnp.concatenate([q_ref[:, cols], qfeat[...]], axis=1)
            scores = lax.dot_general(
                qs, keys[n], (((1,), (1,)), ((), ())), preferred_element_type=f32
            )
            if first:
                qpos = lax.broadcasted_iota(jnp.int32, (tok, tok), 0)
                kpos = lax.broadcasted_iota(jnp.int32, (tok, tok), 1)
                scores = jnp.where(kpos <= qpos, scores, jnp.float32(-1e30))
            top = functools.reduce(
                jnp.maximum,
                [scores[:, i : i + HEAD_SIZE] for i in range(0, blocks * tok, HEAD_SIZE)],
            )
            top = jnp.max(top, axis=1, keepdims=True)
            if not first:
                top = jnp.maximum(top, olds[n][:, 0:1])
            weights = jnp.exp2((scores - top) * factor).astype(bf)
            both = jnp.dot(weights, vals[n], preferred_element_type=f32)
            if not first:
                shrink = jnp.exp2((olds[n] - top) * factor)
                both = accs[n] * jnp.concatenate([shrink, shrink], axis=1) + both
            done.append((jnp.broadcast_to(top, (tok, HEAD_SIZE)), both))
        for head, (top, both) in zip(heads, done):
            rowmax[head] = top
            acc[head] = both

    def attend_some(d, lo, count, s, most):
        for blocks in range(1, most + 1):

            @pl.when(count == blocks)
            def _():
                attend(d, lo, blocks, s, False)

    qfeat[...] = jnp.where(same_lane(0, p), jnp.float32(0.0), jnp.float32(-MASKED)).astype(bf)
    mark(0, p, 1)

    def own_half(s, carry):
        attend(0, p, 1, s, True)
        return carry

    q_in.wait()
    lax.fori_loop(0, 2, own_half, 0)

    @pl.when(z > 0)
    def _():
        for s in range(2):
            kv_wait(1, p, s)

            @pl.when(z < last)
            def _():
                kv_up(1, s).start()

            kv_side(1, 1, s).start()
            kv_side(1, 0, s).start()

        @pl.when(z < last)
        def _():
            w_up(z, 0).start()

        @pl.when(z < helper)
        def _():
            w_up(z, 1).start()

    def first_plane(s, carry):
        def settle(v):
            @pl.when(row == 1)
            def _():
                kv_wait(0, across, v)
                kv_forward(0, v).start()

            @pl.when(core == 1)
            def _():
                kv_wait(0, mate, v)

            @pl.when(row == 1)
            def _():
                kv_wait(0, diag, v)

        each(s, settle)

        @pl.when(s == 0)
        def _():
            mark(0, 0, p)

        attend_some(0, 0, p, s, PLANE - 1)
        return carry

    lax.fori_loop(0, 2, first_plane, 0)

    def second_plane(s, carry):
        @pl.when(z < last)
        def _():
            arrive(z + 1, s)

        def pass_on(v):
            kv_wait(2, p, v)

            @pl.when(row == 1)
            def _():
                kv_side(2, 1, v).start()

            @pl.when(core == 1)
            def _():
                kv_side(2, 0, v).start()

        def settle(v):
            kv_wait(1, across, v)
            kv_forward(1, v).start()
            kv_wait(1, mate, v)
            kv_wait(1, diag, v)

        @pl.when(z > 1)
        def _():
            each(s, pass_on)

        @pl.when(z > 0)
        def _():
            each(s, settle)

            @pl.when(s == 0)
            def _():
                mark(1, 0, PLANE)

            attend(1, 0, PLANE, s, False)

        return carry

    lax.fori_loop(0, 2, second_plane, 0)

    def third_plane(s, carry):
        def settle(v):
            @pl.when(row == 0)
            def _():
                kv_wait(2, across, v)
                kv_forward(2, v).start()

            @pl.when(core == 0)
            def _():
                kv_wait(2, mate, v)

            @pl.when(row == 0)
            def _():
                kv_wait(2, diag, v)

        @pl.when(z > 1)
        def _():
            each(s, settle)

            @pl.when(s == 0)
            def _():
                mark(2, p, PLANE - p)

            attend_some(2, p, PLANE - p, s, PLANE)

        for n in range(part_heads):
            both = acc[s * part_heads + n]
            attn = both[:, 0:HEAD_SIZE] / both[:, HEAD_SIZE : 2 * HEAD_SIZE]
            abuf[p, s, :, n * HEAD_SIZE : (n + 1) * HEAD_SIZE] = attn.astype(bf)
        a_side(1, s).start()
        a_side(0, s).start()

        @pl.when(z == last)
        def _():
            lend_down(p, s, s).start()

        @pl.when((z == helper) & (s == 0))
        def _():
            arrive(z - 1, 0)

        return carry

    lax.fori_loop(0, 2, third_plane, 0)

    def order(i):
        if i == 0:
            return z
        if i == 1:
            return jnp.where(z < last, z + 1, last - 2)
        if i == 2:
            return jnp.where(z == 0, 2, z - 1)
        return jnp.where(z < 2, last, 0)

    def place(u, pp, part):
        mine = ((u // 2) // per_half) == h
        uu = u % (2 * per_half)

        @pl.when(mine)
        def _():
            keep[uu, pp] = part

        @pl.when(jnp.logical_not(mine))
        def _():
            xsend[uu, pp] = part.astype(bf)
            x_copy(uu, pp).start()

    def attn_of(pp):
        return jnp.concatenate([abuf[pp, 0], abuf[pp, 1]], axis=1)

    def project(j, lo, hi):
        def rows(k, carry):
            pp = target(k)
            both = jnp.concatenate([wbuf[j, 0], wbuf[j, 1]], axis=1)
            part = jnp.dot(attn_of(pp), both, preferred_element_type=f32)
            place(2 * j, pp, part[:, :half])
            place(2 * j + 1, pp, part[:, half:])
            return carry

        lax.fori_loop(lo, hi, rows, 0)

    def project_half(j, s):
        def rows(k, carry):
            pp = target(k)
            part = jnp.dot(attn_of(pp), wbuf[j, s], preferred_element_type=f32)
            place(2 * j + s, pp, part)
            return carry

        lax.fori_loop(0, PLANE, rows, 0)

    def project_lent(lo, hi):
        def rows(k, carry):
            pp = target(k)
            rows_of = jnp.concatenate([lent[pp, 0], lent[pp, 1]], axis=1)
            both = jnp.concatenate([wbuf[0, 0], wbuf[0, 1]], axis=1)
            psend[pp] = jnp.dot(rows_of, both, preferred_element_type=f32).astype(bf)
            give_back(pp).start()
            return carry

        lax.fori_loop(lo, hi, rows, 0)

    def take_back(lo, hi):
        def rows(k, carry):
            pp = target(k)
            copy(
                psend.at[pp], precv.at[pp], p_send.at[pp], p_recv.at[pp], in_plane(mate)
            ).wait_recv()
            for s in range(2):
                cols = slice(s * half, (s + 1) * half)

                @pl.when(h == 0)
                def _():
                    keep[s, pp] = precv[pp, :, cols].astype(f32)

                @pl.when(h > 0)
                def _():
                    copy(
                        precv.at[pp, :, cols], xrecv.at[s, pp], x_send.at[s, pp],
                        x_recv.at[s, pp], (1 - h, c),
                    ).start()

            return carry

        lax.fori_loop(lo, hi, rows, 0)

    def settle_rows(u, lo, hi):
        def rows(k, carry):
            pp = target(k)
            x_copy(u, pp).wait_recv()
            rsend[u, pp] = (keep[u, pp] + xrecv[u, pp].astype(f32)).astype(bf)

            @pl.when(pp == p)
            def _():
                o_local(u).start()

            @pl.when(pp != p)
            def _():
                o_copy(u, pp).start()

            return carry

        lax.fori_loop(lo, hi, rows, 0)

    def finish(j, s):
        @pl.when((j // per_half) == h)
        def _():
            settle_rows((2 * j + s) % (2 * per_half), 0, PLANE)

    def finish_rows(lo, hi):
        @pl.when(h == 0)
        def _():
            def one(k, carry):
                def both(s, inner):
                    settle_rows(s, k, k + 1)
                    return inner

                lax.fori_loop(0, 2, both, 0)
                return carry

            lax.fori_loop(lo, hi, one, 0)

    def finish_all(j):
        def one(s, carry):
            finish(j, s)
            return carry

        lax.fori_loop(0, 2, one, 0)

    a_wait(mate, 0)
    a_wait(mate, 1)
    project(order(0), 2, PLANE)

    @pl.when(z < last)
    def _():
        project(order(1), 2, PLANE)

        @pl.when(z < helper)
        def _():
            arrive(order(2), 0)

        arrive(order(2), 1)

        @pl.when(z == helper)
        def _():
            w_up(z, 1).start()

        project(order(2), 2, PLANE)

    @pl.when(z == 1)
    def _():
        arrive(order(3), 0)
        arrive(order(3), 1)

    @pl.when(z == helper)
    def _():
        lend_wait(p, 0)
        lend_mate(p, 0, 0).start()

    a_wait(across, 0)
    a_forward(0).start()

    @pl.when(z == last)
    def _():
        lend_down(across, 0, 2).start()
        arrive(order(1), 0)
        arrive(order(1), 1)

    a_wait(across, 1)
    a_forward(1).start()

    @pl.when(z == helper)
    def _():
        lend_wait(p, 1)
        lend_across().start()
        lend_mate(p, 1, 1).start()

    a_wait(diag, 0)
    a_wait(diag, 1)

    @pl.when(z == last)
    def _():
        project(order(1), 0, PLANE)

    project(order(0), 0, 2)

    @pl.when(z < last)
    def _():
        project(order(1), 0, 2)
        project(order(2), 0, 2)

        @pl.when(z != 1)
        def _():
            arrive(order(3), 0)

        project_half(order(3), 0)

        @pl.when(z == helper)
        def _():
            arrive(order(3), 1)
            lend_wait(mate, 0)
            lend_wait(mate, 1)
            project_lent(2, PLANE)
            lend_wait(across, 0)
            lend_mate(across, 0, 2).start()

        for i in range(PLANE - 1):
            finish_all(order(i))

        @pl.when(z == 0)
        def _():
            arrive(order(3), 1)

        @pl.when(z == helper)
        def _():
            lend_wait(across, 1)
            lend_mate(across, 1, 3).start()
            project_lent(0, 1)
            lend_wait(diag, 0)
            lend_wait(diag, 1)
            project_lent(1, 2)

        project_half(order(3), 1)
        finish_all(order(3))

    @pl.when(z == last)
    def _():
        arrive(order(2), 0)
        project_half(order(2), 0)
        finish_all(order(0))
        arrive(order(2), 1)
        project_half(order(2), 1)
        finish_all(order(1))
        take_back(2, PLANE)
        finish_all(order(2))
        finish_rows(2, PLANE)
        take_back(0, 2)
        finish_rows(0, 2)

    def collect(k, carry):
        u = k // PLANE
        src = k % PLANE

        @pl.when(src != p)
        def _():
            copy(
                rsend.at[u, src], out_ref.at[:, column(u, src)], o_send.at[u, src],
                o_recv.at[u, src], in_plane(mate),
            ).wait_recv()
            o_copy(u, src).wait_send()

        @pl.when(src == p)
        def _():
            o_local(u).wait()

        x_copy(u, src).wait_send()
        return carry

    lax.fori_loop(0, 2 * per_half * PLANE, collect, 0)

    for s in range(2):
        a_side(0, s).wait_send()
        a_side(1, s).wait_send()
        a_forward(s).wait_send()

    @pl.when(z == last)
    def _():
        lend_down(p, 0, 0).wait_send()
        lend_down(p, 1, 1).wait_send()
        lend_down(across, 0, 2).wait_send()

    @pl.when(z == helper)
    def _():
        lend_across().wait_send()
        lend_mate(p, 0, 0).wait_send()
        lend_mate(p, 1, 1).wait_send()
        lend_mate(across, 0, 2).wait_send()
        lend_mate(across, 1, 3).wait_send()
        for pp in range(PLANE):
            give_back(pp).wait_send()

    def w_drain(j, carry):
        @pl.when((j <= z) & ((z < helper) | ((z == helper) & (j > 0))))
        def _():
            w_up(j, 0).wait_send()
            w_up(j, 1).wait_send()

        @pl.when((j >= z) & (z > 0))
        def _():
            w_down(j, 0).wait_send()
            w_down(j, 1).wait_send()

        return carry

    lax.fori_loop(0, planes, w_drain, 0)

    for s in range(2):
        @pl.when(z < last)
        def _():
            kv_up(0, s).wait_send()

            @pl.when(z > 0)
            def _():
                kv_up(1, s).wait_send()

        @pl.when(row == 0)
        def _():
            kv_side(0, 1, s).wait_send()

        @pl.when(core == 0)
        def _():
            kv_side(0, 0, s).wait_send()

        @pl.when(row == 1)
        def _():
            kv_forward(0, s).wait_send()

        @pl.when(z > 0)
        def _():
            kv_side(1, 0, s).wait_send()
            kv_side(1, 1, s).wait_send()
            kv_forward(1, s).wait_send()

        @pl.when(z > 1)
        def _():
            @pl.when(row == 1)
            def _():
                kv_side(2, 1, s).wait_send()

            @pl.when(core == 1)
            def _():
                kv_side(2, 0, s).wait_send()

            @pl.when(row == 0)
            def _():
                kv_forward(2, s).wait_send()


def fused_body(n_ctx, n_heads, queries, keys, values, doc_ids, out_weight):
    tok, qcols = queries.shape
    kdim = keys.shape[1]
    groups = kdim // HEAD_SIZE
    krows, wcols = out_weight.shape
    planes = n_ctx // PLANE
    span = QPG * groups
    per_half = planes // n_heads
    bf, f32 = jnp.bfloat16, jnp.float32
    dma = pltpu.SemaphoreType.DMA
    hbm = functools.partial(pltpu.with_memory_space_constraint, memory_space=pltpu.HBM)
    anywhere = pl.BlockSpec(memory_space=pl.ANY)
    return pl.pallas_call(
        functools.partial(fused_kernel, planes, n_heads, groups, tok, wcols),
        out_shape=jax.ShapeDtypeStruct((tok, per_half * PLANE * wcols), bf),
        in_specs=[pl.BlockSpec(memory_space=pltpu.HBM)] * 5,
        out_specs=anywhere,
        scratch_shapes=[
            pltpu.VMEM((tok, qcols), bf),
            pltpu.VMEM((1, tok), jnp.int32),
            pltpu.VMEM((3, PLANE, 2, tok + DOC_ROWS, kdim), bf),
            pltpu.VMEM((3, PLANE, tok, HEAD_SIZE), bf),
            pltpu.VMEM((tok, HEAD_SIZE), bf),
            pltpu.VMEM((planes, 2, krows, wcols // 2), bf),
            pltpu.VMEM((PLANE, 2, tok, krows // 2), bf),
            pltpu.VMEM((PLANE, 2, tok, krows // 2), bf),
            pltpu.VMEM((span, tok, 2 * HEAD_SIZE), f32),
            pltpu.VMEM((span, tok, HEAD_SIZE), f32),
            pltpu.VMEM((2 * per_half, PLANE, tok, wcols // 2), bf),
            pltpu.VMEM((2 * per_half, PLANE, tok, wcols // 2), bf),
            pltpu.VMEM((2 * per_half, PLANE, tok, wcols // 2), f32),
            pltpu.VMEM((2 * per_half, PLANE, tok, wcols // 2), bf),
            pltpu.VMEM((PLANE, tok, wcols), bf),
            pltpu.VMEM((PLANE, tok, wcols), bf),
            dma((9,)),
            dma((3, PLANE, 2)),
            dma((2, 2)),
            dma((3, 2, 2)),
            dma((3, 2)),
            dma((planes, 2)),
            dma((planes, 2)),
            dma((planes, 2)),
            dma((PLANE, 2)),
            dma((2, 2)),
            dma((2,)),
            dma((2 * per_half, PLANE)),
            dma((2 * per_half, PLANE)),
            dma((2 * per_half, PLANE)),
            dma((2 * per_half, PLANE)),
            dma((PLANE, 2)),
            dma((3,)),
            dma((4,)),
            dma,
            dma((PLANE,)),
            dma((PLANE,)),
            dma((2 * per_half,)),
        ],
        compiler_params=pltpu.CompilerParams(
            collective_id=0, has_side_effects=True, vmem_limit_bytes=44 * 1024 * 1024
        ),
    )(hbm(queries), hbm(doc_ids[None, :]), hbm(keys), hbm(values), hbm(out_weight))


def fits_fused(n_ctx, n_heads, queries, keys, out_weight):
    tokens = queries.shape[0]
    tok = tokens // n_ctx
    reach = min(LOOKBACK_WINDOW, tokens // 2)
    return (
        n_heads == 2
        and n_ctx % PLANE == 0
        and n_ctx // PLANE == 4
        and tok == 2 * HEAD_SIZE
        and reach == 2 * PLANE * tok
        and reach < LOOKBACK_WINDOW
        and keys.shape[1] // n_heads >= tok
        and (out_weight.shape[1] // n_ctx) % 256 == 0
        and keys.shape[1] // n_heads % (2 * HEAD_SIZE) == 0
    )


def passed_along(block, axis, distance):
    devices = range(lax.axis_size(axis))
    route = [(i - distance, i) for i in devices if i - distance in devices]
    return lax.ppermute(block, axis, route)


def body(queries, keys, values, doc_ids, out_weight):
    tok_rows = queries.shape[0]
    groups = keys.shape[1] // HEAD_SIZE
    scale = HEAD_SIZE ** (-0.5)
    q_local = queries.reshape(tok_rows, groups, QPG, HEAD_SIZE)
    here = lax.axis_index("ctx")
    qpos = here * tok_rows + jnp.arange(tok_rows, dtype=jnp.int32)
    reach = LOOKBACK_WINDOW // tok_rows

    def work(state, kblk, vblk, sblk, kstart):
        rowmax, total, accum = state
        scores = (
            jnp.einsum(
                "tgnh,sgh->tgns",
                q_local,
                kblk.reshape(tok_rows, groups, HEAD_SIZE),
                preferred_element_type=jnp.float32,
            )
            * scale
        )
        kpos = kstart + jnp.arange(tok_rows, dtype=jnp.int32)
        vis = (
            (kpos[None, :] <= qpos[:, None])
            & (qpos[:, None] - kpos[None, :] < LOOKBACK_WINDOW)
            & (kpos[None, :] >= 0)
            & (doc_ids[:, None] == sblk[None, :])
        )
        vis = vis[:, None, None, :]
        scores = jnp.where(vis, scores, jnp.float32(-1e30))
        newmax = jnp.maximum(rowmax, jnp.max(scores, axis=-1))
        weights = jnp.where(vis, jnp.exp(scores - newmax[..., None]), jnp.float32(0.0))
        factor = jnp.exp(rowmax - newmax)
        total = total * factor + jnp.sum(weights, axis=-1)
        rounded = weights.astype(jnp.bfloat16)
        contrib = jnp.einsum(
            "tgns,sgh->tgnh",
            rounded,
            vblk.reshape(tok_rows, groups, HEAD_SIZE),
            preferred_element_type=jnp.float32,
        )
        accum = accum * factor[..., None] + contrib
        return (newmax, total, accum)

    def attend(state, kblk, vblk, sblk, kstart):
        return work(state, kblk, vblk, sblk, kstart)

    state = (
        jnp.full((tok_rows, groups, QPG), -1e30, jnp.float32),
        jnp.zeros((tok_rows, groups, QPG), jnp.float32),
        jnp.zeros((tok_rows, groups, QPG, HEAD_SIZE), jnp.float32),
    )
    state = attend(state, keys, values, doc_ids, here * tok_rows)

    def chain_step(depth, carry):
        st, kblk, vblk, sblk = carry
        kblk, vblk, sblk = passed_along((kblk, vblk, sblk), "ctx", 1)
        st = attend(st, kblk, vblk, sblk, (here - depth) * tok_rows)
        return (st, kblk, vblk, sblk)

    state = lax.fori_loop(1, reach + 1, chain_step, (state, keys, values, doc_ids))[0]
    rowmax, total, accum = state
    attn = (
        (accum / total[..., None]).astype(jnp.bfloat16).reshape(tok_rows, groups * QPG * HEAD_SIZE)
    )
    partial_sums = jnp.dot(
        attn,
        lax.all_gather(out_weight, "ctx", axis=1, tiled=True),
        preferred_element_type=jnp.float32,
    )
    return lax.psum_scatter(
        partial_sums.astype(jnp.bfloat16), "heads", scatter_dimension=1, tiled=True
    )


def solution(mesh):
    in_specs = (
        P("ctx", "heads"),
        P("ctx", "heads"),
        P("ctx", "heads"),
        P("ctx"),
        P("heads", "ctx"),
    )
    out_specs = P("ctx", "heads")

    def run(queries, keys, values, doc_ids, out_weight):
        n_ctx, n_heads = mesh.shape["ctx"], mesh.shape["heads"]
        local = body
        if fits_fused(n_ctx, n_heads, queries, keys, out_weight):
            local = functools.partial(fused_body, n_ctx, n_heads)
        return jax.shard_map(
            local, mesh=mesh, in_specs=in_specs, out_specs=out_specs, check_vma=False
        )(queries, keys, values, doc_ids, out_weight)

    return run
```
